512 devices in a mesh: ctx: 4 (over z_hi), row: 8 (over x, core), col: 16 (over y, z_lo).
Axes of the slice: x: 4, y: 8, z: 8 (z_hi: 4, z_lo: 2; z = z_hi * 2 + z_lo), core: 2. Of those that a mesh axis runs over, the one named last changes fastest.
Arguments:
- tokens: bfloat16 [1024, 8192], P('ctx', 'row'), may hold values from -6 to 6
- proj_x: bfloat16 [8192, 8192], P('row', 'col'), may hold values from -0.09375 to 0.09375
- proj_z: bfloat16 [8192, 8192], P('row', 'col'), may hold values from -0.0625 to 0.0625
- proj_bc: bfloat16 [8192, 256], P('row'), may hold values from -0.015625 to 0.015625
- proj_dt: bfloat16 [8192, 128], P('row', 'col'), may hold values from -0.0625 to 0.0625
- dt_bias: float32 [128], P('col'), may hold values from -1.5 to 0.5
- decay_rate: float32 [128], P('col'), may hold values from 0.00048828125 to 0.2
- skip_gain: float32 [128], P('col'), may hold values from 0.5 to 1.5
- conv_x: float32 [8192, 4], P('col'), may hold values from -3 to 3
- conv_bc: float32 [256, 4], replicated, may hold values from -3 to 3
- norm_gain: float32 [8192], P('col'), may hold values from 0.1 to 1.9
- proj_out: bfloat16 [8192, 8192], P('col', 'row'), may hold values from -0.09375 to 0.09375
Outputs:
- layer_out: bfloat16 [1024, 8192], P('ctx', ('row', 'col'))
The draws below stay inside these ranges and needn't reach their ends.
All inputs are finite; a program needn't handle non-finite values.
Results may differ from the reference program's by a relative error of at most 0.03.
Values may be sent and summed in bfloat16 or wider, within the bound.
A program may use at most 64 MiB of HBM per device.

```python
import math
import jax
import jax.numpy as jnp
from jax import lax

D = 8192
H = 128
P_SIZE = 64
N = 128
Q = 256
K = 4
INNER = 8192
TOKENS = 1024
N_ROW = 8


def raised(entries, key, source, target, parts, factor):
    owner, partner = [(jnp.arange(entries.shape[dim]) // (entries.shape[dim] // parts)).reshape([-1 if axis == dim else 1 for axis in range(entries.ndim)]) for dim in (source, target)]
    chosen = jax.random.permutation(key, parts)[partner]
    strong = (owner == chosen) | (owner == (partner + parts // 2) % parts)
    return jnp.where(strong, factor * entries, entries)


def level_of(key, dims, pieces, least, largest):
    gain, own = 1.0, jax.random.fold_in(key, 6)
    for position, blocks in pieces:
        steps = jnp.exp(jax.random.uniform(jax.random.fold_in(own, position), (blocks,), jnp.float32, least / len(pieces), largest / len(pieces)))
        gain = gain * jnp.repeat(steps, dims[position] // blocks).reshape([-1 if axis == position else 1 for axis in range(len(dims))])
    return gain


def scatter_about(own_key, dims, scale, reach, cuts=(), kind=jnp.bfloat16):
    loudness = level_of(own_key, dims, cuts, -0.22, 0.18) if cuts else 1.0
    result = jax.random.normal(own_key, dims, jnp.float32) * scale * loudness
    return jnp.minimum(jnp.maximum(result, -reach), reach).astype(kind)


def bell_draw_with(key, dims, spread, limit, cuts, heavy, dtype=jnp.bfloat16):
    values = spread * jax.random.normal(key, dims, jnp.float32)
    if cuts:
        values = values * level_of(key, dims, cuts, -0.22, 0.18)
    return jnp.clip(raised(values, jax.random.fold_in(key, 3), *heavy), -limit, limit).astype(dtype)


def setup_inputs(seed: int = 0) -> dict:
    key_of = jax.random.split(jax.random.key(seed), 13)
    return {
        "tokens": scatter_about(key_of[0], (TOKENS, D), 1.0, 6.0, ((0, 4), (1, 8))),
        "proj_x": bell_draw_with(key_of[1], (D, INNER), D ** -0.5, 0.09375, ((0, 8), (1, 16)), (0, 1, 16, 2.0)),
        "proj_z": scatter_about(key_of[2], (D, INNER), D ** -0.5, 0.0625, ((0, 8), (1, 16))),
        "proj_bc": scatter_about(key_of[3], (D, 2 * N), (0.25 * D ** -0.5), 0.015625, ((0, 8),)),
        "proj_dt": scatter_about(key_of[4], (D, H), D ** -0.5, 0.0625, ((0, 8), (1, 16))),
        "dt_bias": jnp.clip(-1.5 + 2.0 * jax.random.uniform(key_of[5], (H,), jnp.float32) ** level_of(key_of[5], (H,), ((0, 16),), -0.2, 0.2), -1.5, 0.5),
        "decay_rate": jnp.clip(jnp.exp(math.log(0.2) - 6.015181 * jax.random.uniform(key_of[6], (H,), jnp.float32) ** level_of(key_of[6], (H,), ((0, 16),), -0.2, 0.2)), 0.00048828125, 0.2),
        "skip_gain": jnp.clip(0.5 + 1.0 * jax.random.uniform(key_of[7], (H,), jnp.float32) ** level_of(key_of[7], (H,), ((0, 16),), -0.2, 0.2), 0.5, 1.5),
        "conv_x": scatter_about(key_of[8], (INNER, K), K ** -0.5, 3.0, ((0, 16),), jnp.float32),
        "conv_bc": scatter_about(key_of[9], (2 * N, K), K ** -0.5, 3.0, (), jnp.float32),
        "norm_gain": jnp.clip(1.0 + 0.18 * jax.random.normal(key_of[10], (INNER,), jnp.float32), 0.1, 1.9),
        "proj_out": bell_draw_with(key_of[11], (INNER, D), INNER ** -0.5, 0.09375, ((0, 16), (1, 8)), (0, 1, 16, 2.0)),
    }


highest_mode = lax.Precision.HIGHEST

def blocked_product(tokens, weight):
    block_width = tokens.shape[1] // N_ROW
    running = jnp.zeros((tokens.shape[0], weight.shape[1]), jnp.float32)
    for block_index in range(N_ROW):
        low_edge = block_index * block_width
        block_sum = jnp.dot(tokens[:, low_edge:low_edge + block_width], weight[low_edge:low_edge + block_width], preferred_element_type=jnp.float32)
        rounded = lax.optimization_barrier(block_sum.astype(jnp.bfloat16))
        running = running + rounded.astype(jnp.float32)
    return running.astype(jnp.bfloat16)

def causal_conv(values, kernel):
    tap_count = kernel.shape[1]
    padded = jnp.pad(values.astype(jnp.float32), ((tap_count - 1, 0), (0, 0)))
    running = jnp.zeros(values.shape, jnp.float32)
    for tap_index in range(tap_count):
        running = running + kernel[:, tap_index] * padded[tap_index:tap_index + values.shape[0]]
    return jax.nn.silu(running)

def head_scan(inputs_now, b_full, c_full):
    x_head, dt_head, decay_now, skip_now = inputs_now
    seq_len = x_head.shape[0]
    group_count = seq_len // Q
    log_decay = (-decay_now * dt_head).reshape(group_count, Q)
    cum_decay = jnp.cumsum(log_decay, axis=1)
    x_scaled = (x_head * dt_head[:, None]).reshape(group_count, Q, -1)
    b_blocks = b_full.reshape(group_count, Q, -1)
    c_blocks = c_full.reshape(group_count, Q, -1)
    scores = jnp.einsum('cin,cjn->cij', c_blocks, b_blocks, precision=highest_mode)
    lower_mask = jnp.arange(Q)[:, None] >= jnp.arange(Q)[None, :]
    log_gap = cum_decay[:, :, None] - cum_decay[:, None, :]
    weights = jnp.where(lower_mask, jnp.exp(jnp.where(lower_mask, log_gap, 0.0)), 0.0)
    inner_out = jnp.einsum('cij,cjp->cip', scores * weights, x_scaled, precision=highest_mode)
    tail_weight = jnp.exp(cum_decay[:, -1:] - cum_decay)
    group_states = jnp.einsum('cj,cjp,cjn->cpn', tail_weight, x_scaled, b_blocks, precision=highest_mode)

    def group_step(carried, step_inputs):
        group_log, group_state = step_inputs
        return (jnp.exp(group_log) * carried + group_state, carried)
    start_state = jnp.zeros(group_states.shape[1:], jnp.float32)
    final_state, entering = lax.scan(group_step, start_state, (cum_decay[:, -1], group_states))
    outer_out = jnp.exp(cum_decay)[:, :, None] * jnp.einsum('cin,cpn->cip', c_blocks, entering, precision=highest_mode)
    return (inner_out + outer_out).reshape(seq_len, -1) + skip_now * x_head

def reference(tokens, proj_x, proj_z, proj_bc, proj_dt, dt_bias, decay_rate, skip_gain, conv_x, conv_bc, norm_gain, proj_out):
    x_in = blocked_product(tokens, proj_x)
    z_in = blocked_product(tokens, proj_z)
    bc_in = blocked_product(tokens, proj_bc)
    dt_in = blocked_product(tokens, proj_dt)
    x_conv = causal_conv(x_in, conv_x)
    bc_conv = causal_conv(bc_in, conv_bc)
    b_full = bc_conv[:, :N]
    c_full = bc_conv[:, N:]
    dt_full = jax.nn.softplus(dt_in.astype(jnp.float32) + dt_bias)
    seq_len = tokens.shape[0]
    x_heads = x_conv.reshape(seq_len, H, P_SIZE).transpose(1, 0, 2)
    ssm_heads = lax.map(lambda inputs_now: head_scan(inputs_now, b_full, c_full), (x_heads, dt_full.T, decay_rate, skip_gain))
    ssm_out = ssm_heads.transpose(1, 0, 2)
    gated = ssm_out * jax.nn.silu(z_in.astype(jnp.float32)).reshape(seq_len, H, P_SIZE)
    inv_rms = lax.rsqrt(lax.optimization_barrier(jnp.mean(gated * gated, axis=2, keepdims=True)) + 1e-05)
    normed = (gated * inv_rms * norm_gain.reshape(H, P_SIZE)).reshape(seq_len, H * P_SIZE).astype(jnp.bfloat16)
    return jnp.dot(normed, proj_out, preferred_element_type=jnp.float32).astype(jnp.bfloat16)
```

```python
import functools

import jax
import jax.numpy as jnp
from jax import lax
from jax.experimental import pallas as pl
from jax.experimental.pallas import tpu as pltpu
from jax.sharding import PartitionSpec as P

MESH = pl.DeviceIdType.MESH
F32 = jnp.float32
BF16 = jnp.bfloat16

N_CTX, N_ROW, N_COL = 4, 8, 16
N_X, N_Y = 4, 8
T = 256
KB = 1024
HD = 64
SLAB = 2 * HD + 16
TB = T // N_ROW
HAL = 8
FAR_FIRST_X = (2, 1, 3)
FAR_FIRST_Y = (4, 3, 5, 2, 6, 1, 7)


def dot(a, b):
    return jnp.dot(a, b, preferred_element_type=F32)


def dot_t(a, b):
    return lax.dot_general(a, b, (((1,), (1,)), ((), ())), preferred_element_type=F32)


def iota(shape, dim):
    return lax.broadcasted_iota(jnp.int32, shape, dim)


def silu(v):
    return v / (1.0 + jnp.exp(-v))


def kernel(
    tok_h, wx_h, wz_h, wbc_h, wdt_h, wout_h, cx_h, cbc_h, gain_h,
    bias_s, decay_s, skip_s,
    out_ref,
    tok, hal, wx, wz, wbc, wdt, wout, cx, cbc, gain,
    eye, tril, prm, prmt, wt,
    pbc, pxz, abc, axz, sbc, sxz, rbc, rxz, hs, hr, bcraw, bcf,
    st, sr, nb, os, ow, zr, ys, yr,
    sem_l, sem_hal,
    abc_s, abc_r, axz_s, axz_r, sbc_s, sbc_r, sxz_s, sxz_r, hr_s, hr_r,
    gbc_s, gbc_r, st_s, st_r, gn_s, gn_r, z_s, z_r, y_s, y_r,
):
    ctx = lax.axis_index("ctx")
    row = lax.axis_index("row")
    col = lax.axis_index("col")
    x, core = row // 2, row % 2
    y, zl = col // 2, col % 2

    def remote(src, dst, ss, rs, **peer):
        return pltpu.make_async_remote_copy(
            src_ref=src, dst_ref=dst, send_sem=ss, recv_sem=rs,
            device_id=peer, device_id_type=MESH,
        )

    barrier = pltpu.get_barrier_semaphore()

    def greet(**peer):
        pl.semaphore_signal(barrier, inc=1, device_id=peer, device_id_type=MESH)

    for d in range(1, N_CTX):
        greet(ctx=(ctx + d) % N_CTX)
    for d in FAR_FIRST_Y:
        greet(col=((y + d) % N_Y) * 2 + zl)
    for d in range(1, N_ROW):
        greet(row=(row + d) % N_ROW)
    greet(col=col + 1 - 2 * zl)

    loads = [
        pltpu.make_async_copy(src, dst, sem_l.at[k])
        for k, (src, dst) in enumerate(
            (
                (tok_h, tok), (wbc_h, wbc), (wx_h, wx), (wz_h, wz), (wdt_h, wdt),
                (wout_h, wout), (cx_h, cx), (cbc_h, cbc), (gain_h, gain),
            )
        )
    ]
    for load in loads:
        load.start()

    eye[...] = jnp.where(iota((T, T), 0) == iota((T, T), 1), 1.0, 0.0).astype(BF16)
    tril[...] = jnp.where(iota((T, T), 0) >= iota((T, T), 1), 1.0, 0.0).astype(BF16)
    prm[...] = jnp.zeros(prm.shape, F32)

    loads[0].wait()
    loads[1].wait()
    pbc[...] = dot(tok[...], wbc[...]).astype(BF16).reshape(N_ROW, TB, T)
    loads[4].wait()
    dt_part = dot_t(wdt[...], tok[...])
    for h in range(N_ROW):
        pxz[h, 2 * HD :, :] = jnp.broadcast_to(dt_part[h : h + 1], (16, T)).astype(BF16)
    for k, w in ((2, wx), (3, wz)):
        loads[k].wait()
        for b in range(2):
            part = dot(tok[...], w[:, b * T : (b + 1) * T]).astype(BF16)
            part = dot_t(eye[...], part).astype(BF16)
            for h in range(4):
                at = (k - 2) * HD
                pxz[4 * b + h, at : at + HD, :] = part[h * HD : (h + 1) * HD]

    pl.semaphore_wait(barrier, N_CTX - 1 + N_Y - 1 + N_ROW - 1 + 1)

    send_hal = remote(
        tok.at[pl.ds(T - HAL, HAL)], hal, sem_hal.at[0], sem_hal.at[1],
        ctx=(ctx + 1) % N_CTX,
    )

    @pl.when(ctx + 1 < N_CTX)
    def _():
        send_hal.start()

    def chip(d):
        return (x + d) % N_X

    order_a = FAR_FIRST_X + (0,)
    copies_abc = {
        d: remote(pbc.at[2 * chip(d) + 1 - core], abc.at[d], abc_s.at[d], abc_r.at[d], row=2 * x + 1 - core)
        for d in order_a
    }
    copies_axz = {
        d: remote(pxz.at[2 * chip(d) + 1 - core], axz.at[d], axz_s.at[d], axz_r.at[d], row=2 * x + 1 - core)
        for d in order_a
    }
    for d in order_a:
        copies_abc[d].start()
    for d in order_a:
        copies_axz[d].start()

    copies_sbc, copies_sxz = {}, {}
    for d in FAR_FIRST_X:
        copies_abc[d].wait_recv()
        sbc[d] = (pbc[2 * chip(d) + core].astype(F32) + abc[d].astype(F32)).astype(BF16)
        copies_sbc[d] = remote(sbc.at[d], rbc.at[d], sbc_s.at[d], sbc_r.at[d], row=2 * chip(d) + core)
        copies_sbc[d].start()
    for d in FAR_FIRST_X:
        copies_axz[d].wait_recv()
        sxz[d] = (pxz[2 * chip(d) + core].astype(F32) + axz[d].astype(F32)).astype(BF16)
        copies_sxz[d] = remote(sxz.at[d], rxz.at[d], sxz_s.at[d], sxz_r.at[d], row=2 * chip(d) + core)
        copies_sxz[d].start()

    @pl.when(ctx == 0)
    def _():
        hal[...] = jnp.zeros(hal.shape, BF16)

    @pl.when(ctx > 0)
    def _():
        send_hal.wait_recv()

    hal_bc = dot(hal[...], wbc[...]).astype(BF16)
    hal_x = dot(hal[...], wx[...]).astype(BF16)
    for b in range(2):
        hs[b, :HAL] = hal_bc
        hs[b, HAL:] = hal_x[:, b * T : (b + 1) * T]
    hr[row] = hs[row // 4]
    copies_hr = {}
    for d in range(1, N_ROW):
        to = (row + d) % N_ROW
        copies_hr[d] = remote(hs.at[to // 4], hr.at[row], hr_s.at[d], hr_r.at[d], row=to)
        copies_hr[d].start()

    copies_abc[0].wait_recv()
    bc_sum = pbc[row].astype(F32) + abc[0].astype(F32)
    for d in FAR_FIRST_X:
        copies_sbc[d].wait_recv()
        bc_sum += rbc[d].astype(F32)
    bcraw[row] = bc_sum.astype(BF16)
    copies_gbc = {}
    for d in range(1, N_ROW):
        copies_gbc[d] = remote(
            bcraw.at[row], bcraw.at[row], gbc_s.at[d], gbc_r.at[d], row=(row + d) % N_ROW
        )
        copies_gbc[d].start()

    for k in (6, 7, 8):
        loads[k].wait()
    lanes = pl.ds(pl.multiple_of((row // 2) * 128, 128), 128)
    prm[0:4, :] = cx[:, lanes]
    prm[4:5, :] = gain[:, lanes]
    prmt[...] = prm[...].T
    col_prm = prmt[pl.ds(pl.multiple_of((row % 2) * HD, HD), HD), :]

    loads[5].wait()
    for nb_ in range(4):
        for kb in range(2):
            block = dot_t(eye[...], wout[kb * T : (kb + 1) * T, nb_ * T : (nb_ + 1) * T]).astype(BF16)
            for s in range(4):
                wt[s % 2, 2 * nb_ + s // 2, :, kb * T : (kb + 1) * T] = block[s * HD : (s + 1) * HD]

    copies_axz[0].wait_recv()
    xz = pxz[row].astype(F32) + axz[0].astype(F32)
    for d in FAR_FIRST_X:
        copies_sxz[d].wait_recv()
        xz += rxz[d].astype(F32)
    x_in = xz[:HD]
    z_in = xz[HD : 2 * HD]
    dt_v = xz[2 * HD : 2 * HD + 8] + bias_s[row]
    dt8 = jnp.maximum(dt_v, 0.0) + jnp.log1p(jnp.exp(-jnp.abs(dt_v)))
    dt_row = dt8[0:1]

    log8 = dt8 * (-decay_s[row])
    hi = log8.astype(BF16).astype(F32)
    mid = (log8 - hi).astype(BF16).astype(F32)
    low = log8 - hi - mid
    sub = iota((8, T), 0)
    three = jnp.where(sub == 0, hi, jnp.where(sub == 1, mid, jnp.where(sub == 2, low, 0.0))).astype(BF16)
    cum_row = jnp.sum(dot_t(three, tril[...]), axis=0, keepdims=True)
    cum_col = jnp.sum(dot_t(tril[...], three), axis=1, keepdims=True)
    total = cum_row[:, T - 1 :]
    tail = jnp.exp(total - cum_row)
    gap = cum_col - cum_row
    keep = iota((T, T), 0) >= iota((T, T), 1)
    weights = jnp.where(keep, jnp.exp(jnp.where(keep, gap, 0.0)), 0.0)

    for d in range(1, N_ROW):
        copies_hr[d].wait_recv()
    halo = hr[0].astype(F32)
    for s in range(1, N_ROW):
        halo += hr[s].astype(F32)
    pick = jnp.where(iota((HD, T), 1) == (row % 4) * HD + iota((HD, T), 0), 1.0, 0.0).astype(BF16)
    before = jnp.concatenate([jnp.zeros((128 - HAL, T), F32), halo[HAL:]], axis=0).astype(BF16)
    x_before = dot_t(pick, before)

    x_cat = jnp.concatenate([x_before, x_in], axis=1)
    acc = col_prm[:, 3:4] * x_in
    for k in range(3):
        acc += col_prm[:, k : k + 1] * pltpu.roll(x_cat, 3 - k, 1)[:, 128:]
    x_conv = silu(acc)
    xs = x_conv * dt_row

    for d in range(1, N_ROW):
        copies_gbc[d].wait_recv()
    bcf[:HAL] = halo[:HAL]
    bcf[HAL:] = bcraw[...].reshape(T, T).astype(F32)
    acc = cbc[3:4, :] * bcf[HAL : HAL + T]
    for k in range(3):
        acc += cbc[k : k + 1, :] * bcf[HAL - 3 + k : HAL - 3 + k + T]
    bc_conv = silu(acc).astype(BF16)
    b_mat, c_mat = bc_conv[:, :128], bc_conv[:, 128:]

    state = dot((xs * tail).astype(BF16), b_mat)
    st[:HD] = state.astype(BF16)
    total_hi = total.astype(BF16).astype(F32)
    st[HD : HD + 8] = jnp.broadcast_to(total_hi, (8, 128)).astype(BF16)
    st[HD + 8 :] = jnp.broadcast_to(total - total_hi, (8, 128)).astype(BF16)
    copies_st = {
        d: remote(st, sr.at[d], st_s.at[d], st_r.at[d], ctx=(ctx + d) % N_CTX)
        for d in range(1, N_CTX)
    }
    for d in (2, 3, 1):
        @pl.when(ctx + d < N_CTX)
        def _():
            copies_st[d].start()

        @pl.when(ctx < d)
        def _():
            sr[d] = jnp.zeros(sr.shape[1:], BF16)

    scores = dot_t(c_mat, b_mat)
    inner = dot_t(xs.astype(BF16), (scores * weights).astype(BF16))
    partial_out = inner + skip_s[row] * x_conv
    gate = silu(z_in)
    for d in (1, 3, 2):
        @pl.when(ctx >= d)
        def _():
            copies_st[d].wait_recv()

    def log_of(d):
        return (sr[d, HD : HD + 8].astype(F32) + sr[d, HD + 8 :].astype(F32))[0:1]

    enter = sr[1, :HD].astype(F32)
    enter += jnp.exp(log_of(1)) * sr[2, :HD].astype(F32)
    enter += jnp.exp(log_of(1) + log_of(2)) * sr[3, :HD].astype(F32)
    outer = dot_t(enter.astype(BF16), c_mat) * jnp.exp(cum_row)
    gated = (partial_out + outer) * gate
    inv = lax.rsqrt(jnp.sum(gated * gated, axis=0, keepdims=True) * (1.0 / HD) + 1e-05)
    nb[row] = (gated * inv * col_prm[:, 4:5]).astype(BF16)

    copies_gn = {}
    for d in range(1, N_ROW):
        copies_gn[d] = remote(nb.at[row], nb.at[row], gn_s.at[d], gn_r.at[d], row=(row + d) % N_ROW)
        copies_gn[d].start()
    for d in range(1, N_ROW):
        copies_gn[d].wait_recv()

    heads = nb[...].reshape(N_ROW * HD, T)
    os[...] = dot(wt[1 - zl].reshape(N_Y * HD, N_ROW * HD), heads).astype(BF16).reshape(N_Y, HD, T)
    copies_z, copies_y = {}, {}
    for d in FAR_FIRST_Y + (0,):
        copies_z[d] = remote(
            os.at[(y + d) % N_Y], zr.at[d], z_s.at[d], z_r.at[d], col=col + 1 - 2 * zl
        )
        copies_z[d].start()
    ow[...] = dot(wt[zl].reshape(N_Y * HD, N_ROW * HD), heads).astype(BF16).reshape(N_Y, HD, T)
    for d in FAR_FIRST_Y:
        copies_z[d].wait_recv()
        ys[d] = (ow[(y + d) % N_Y].astype(F32) + zr[d].astype(F32)).astype(BF16)
        copies_y[d] = remote(ys.at[d], yr.at[d], y_s.at[d], y_r.at[d], col=((y + d) % N_Y) * 2 + zl)
        copies_y[d].start()
    copies_z[0].wait_recv()
    result = ow[y].astype(F32) + zr[0].astype(F32)
    for d in FAR_FIRST_Y:
        copies_y[d].wait_recv()
        result += yr[d].astype(F32)
    out_ref[...] = result.astype(BF16)

    @pl.when(ctx + 1 < N_CTX)
    def _():
        send_hal.wait_send()

    for d in range(1, N_CTX):
        @pl.when(ctx + d < N_CTX)
        def _():
            copies_st[d].wait_send()

    for group in (copies_abc, copies_axz, copies_sbc, copies_sxz, copies_hr, copies_gbc, copies_gn, copies_z, copies_y):
        for copy in group.values():
            copy.wait_send()


def scratch():
    vmem = pltpu.VMEM
    dma = lambda n: pltpu.SemaphoreType.DMA((n,))
    return [
        vmem((T, KB), BF16), vmem((HAL, KB), BF16), vmem((KB, 512), BF16), vmem((KB, 512), BF16),
        vmem((KB, 256), BF16), vmem((8, KB), BF16), vmem((512, KB), BF16),
        vmem((4, 512), F32), vmem((4, 256), F32), vmem((1, 512), F32),
        vmem((T, T), BF16), vmem((T, T), BF16), vmem((128, 128), F32), vmem((128, 128), F32),
        vmem((2, N_Y, HD, 512), BF16),
        vmem((N_ROW, TB, T), BF16), vmem((N_ROW, SLAB, T), BF16),
        vmem((N_X, TB, T), BF16), vmem((N_X, SLAB, T), BF16),
        vmem((N_X, TB, T), BF16), vmem((N_X, SLAB, T), BF16),
        vmem((N_X, TB, T), BF16), vmem((N_X, SLAB, T), BF16),
        vmem((2, 2 * HAL, T), BF16), vmem((N_ROW, 2 * HAL, T), BF16),
        vmem((N_ROW, TB, T), BF16), vmem((HAL + T, T), F32),
        vmem((HD + 16, 128), BF16), vmem((N_CTX, HD + 16, 128), BF16),
        vmem((N_ROW, HD, T), BF16), vmem((N_Y, HD, T), BF16), vmem((N_Y, HD, T), BF16),
        vmem((N_Y, HD, T), BF16), vmem((N_Y, HD, T), BF16), vmem((N_Y, HD, T), BF16),
        dma(9), dma(2),
        dma(4), dma(4), dma(4), dma(4), dma(4), dma(4), dma(4), dma(4), dma(8), dma(8),
        dma(8), dma(8), dma(4), dma(4), dma(8), dma(8), dma(8), dma(8), dma(8), dma(8),
    ]


def local(tokens, proj_x, proj_z, proj_bc, proj_dt, dt_bias, decay_rate, skip_gain, conv_x, conv_bc, norm_gain, proj_out):
    hbm = pl.BlockSpec(memory_space=pl.ANY)
    smem = pl.BlockSpec(memory_space=pltpu.SMEM)
    out = pl.pallas_call(
        kernel,
        out_shape=jax.ShapeDtypeStruct((HD, T), BF16),
        in_specs=[hbm] * 9 + [smem] * 3,
        out_specs=pl.BlockSpec(memory_space=pltpu.VMEM),
        scratch_shapes=scratch(),
        compiler_params=pltpu.CompilerParams(collective_id=0, has_side_effects=True),
    )(
        tokens, proj_x, proj_z, proj_bc, proj_dt.T, proj_out,
        conv_x.T, conv_bc.T, norm_gain.reshape(1, -1),
        dt_bias, decay_rate, skip_gain,
    )
    return out.T


def solution(mesh):
    in_specs = (
        P("ctx", "row"),
        P("row", "col"),
        P("row", "col"),
        P("row", None),
        P("row", "col"),
        P("col"),
        P("col"),
        P("col"),
        P("col", None),
        P(),
        P("col"),
        P("col", "row"),
    )
    out_specs = P("ctx", ("row", "col"))
    return jax.shard_map(local, mesh=mesh, in_specs=in_specs, out_specs=out_specs, check_vma=False)
```

```python
import functools

import jax
import jax.numpy as jnp
from jax import lax
from jax.experimental import pallas as pl
from jax.experimental.pallas import tpu as pltpu
from jax.sharding import PartitionSpec as P

MESH = pl.DeviceIdType.MESH
F32 = jnp.float32
BF16 = jnp.bfloat16

N_CTX, N_ROW, N_COL = 4, 8, 16
N_X, N_Y = 4, 8
T = 256
KB = 1024
HD = 64
TB = T // N_ROW
HAL = 16
FAR_FIRST_Y = (4, 3, 5, 2, 6, 1, 7)


def dot(a, b):
    return jnp.dot(a, b, preferred_element_type=F32)


def dot_t(a, b):
    return lax.dot_general(a, b, (((1,), (1,)), ((), ())), preferred_element_type=F32)


def iota(shape, dim):
    return lax.broadcasted_iota(jnp.int32, shape, dim)


def silu(v):
    return v / (1.0 + jnp.exp(-v))


class Links:
    def __init__(self):
        self.started = []

    def when(self, cond, act):
        if cond is None:
            act()
        else:
            pl.when(cond)(act)

    def start(self, copy, cond_send=None, cond_recv=None):
        self.when(cond_send, copy.start)
        self.started.append([copy, cond_send, cond_recv, True])
        return len(self.started) - 1

    def arrive(self, k):
        copy, _, cond, waiting = self.started[k]
        if waiting:
            self.when(cond, copy.wait_recv)
            self.started[k][3] = False

    def finish(self):
        for k, (copy, cond, _, _) in enumerate(self.started):
            self.arrive(k)
            self.when(cond, copy.wait_send)


def kernel(
    tok_h, wx_h, wz_h, wbc_h, wdt_h, wout_h, cx_h, cbc_h, gain_h,
    bias_s, decay_s, skip_s,
    out_ref,
    tok, wx, wz, wbc, wdt, wout, cx, cbc, gain,
    eye, tril, prm, prmt, wt,
    pbc, px, pz, abc, ax, az, sbc, sx, sz, rbc, rx, rz, xt, xt_in, bt_in, bcraw, bcf,
    st, sr, nb, os, ow, zr, ys, yr,
    here_y, here_ctx, sem_l, tail_s, tail_r,
    abc_s, abc_r, ax_s, ax_r, az_s, az_r, sbc_s, sbc_r, sx_s, sx_r, sz_s, sz_r,
    gbc_s, gbc_r, st_s, st_r, gn_s, gn_r, z_s, z_r, y_s, y_r,
):
    ctx = lax.axis_index("ctx")
    row = lax.axis_index("row")
    col = lax.axis_index("col")
    x, core = row // 2, row % 2
    y, zl = col // 2, col % 2

    def remote(src, dst, ss, rs, **peer):
        return pltpu.make_async_remote_copy(
            src_ref=src, dst_ref=dst, send_sem=ss, recv_sem=rs,
            device_id=peer, device_id_type=MESH,
        )

    barrier = pltpu.get_barrier_semaphore()

    def greet(**peer):
        pl.semaphore_signal(barrier, inc=1, device_id=peer, device_id_type=MESH)

    def rank(at):
        return jnp.minimum(at, N_Y - at) * N_Y + at

    waits = N_ROW - 1 + 1 + ctx
    for d in range(1, N_ROW):
        greet(row=(row + d) % N_ROW)
    greet(col=col + 1 - 2 * zl)
    earlier = {}
    for d in range(1, N_Y):
        peer = (y + d) % N_Y
        earlier[d] = rank(peer) < rank(y)
        waits += earlier[d].astype(jnp.int32)
        pl.when(jnp.logical_not(earlier[d]))(lambda: greet(col=peer * 2 + zl))
    for d in range(1, N_CTX):
        pl.when(ctx + d < N_CTX)(lambda: greet(ctx=ctx + d))

    def enter():
        pl.semaphore_wait(barrier, waits)
        for d in range(1, N_Y):
            peer = ((y + d) % N_Y) * 2 + zl
            pl.when(earlier[d])(
                lambda: pl.semaphore_signal(here_y, inc=1, device_id={"col": peer}, device_id_type=MESH)
            )
        for d in range(1, N_CTX):
            pl.when(ctx >= d)(
                lambda: pl.semaphore_signal(here_ctx.at[d], inc=1, device_id={"ctx": ctx - d}, device_id_type=MESH)
            )

    def present_y():
        if not seen["y"]:
            seen["y"] = True
            later = N_Y - 1 - (waits - N_ROW - ctx)
            pl.when(later > 0)(lambda: pl.semaphore_wait(here_y, later))

    def present_ctx(d):
        if d not in seen:
            seen[d] = True
            pl.when(ctx + d < N_CTX)(lambda: pl.semaphore_wait(here_ctx.at[d], 1))

    seen = {"y": False}
    b0 = ((x + 2) % N_X) // 2
    cols_of = lambda b: pl.ds(pl.multiple_of(b * T, T), T)
    loads = [
        pltpu.make_async_copy(src, dst, sem_l.at[k])
        for k, (src, dst) in enumerate(
            (
                (tok_h, tok), (wbc_h, wbc), (wdt_h, wdt),
                (wx_h.at[:, cols_of(b0)], wx.at[0]), (wx_h.at[:, cols_of(1 - b0)], wx.at[1]),
                (wz_h.at[:, cols_of(b0)], wz.at[0]), (wz_h.at[:, cols_of(1 - b0)], wz.at[1]),
                (cx_h, cx), (cbc_h, cbc), (gain_h, gain), (wout_h, wout),
            )
        )
    ]
    links = Links()
    pending = set()

    def fetch(*ks):
        for k in ks:
            pending.add(k)
            loads[k].start()

    fetch(0, 1, 2, 3, 4)

    def need(*ks):
        for k in ks:
            if k in pending:
                pending.remove(k)
                loads[k].wait()

    def done():
        need(*tuple(pending))
        present_y()
        for d in range(1, N_CTX):
            present_ctx(d)
        links.finish()

    eye[...] = jnp.where(iota((T, T), 0) == iota((T, T), 1), 1.0, 0.0).astype(BF16)
    tril[...] = jnp.where(iota((T, T), 0) >= iota((T, T), 1), 1.0, 0.0).astype(BF16)
    prm[...] = jnp.zeros(prm.shape, F32)

    need(0, 1)
    pbc[...] = dot(tok[...], wbc[...]).astype(BF16).reshape(N_ROW, TB, T)
    fetch(5, 6, 7, 8, 9)
    need(2)
    dt_part = dot_t(wdt[...], tok[...])
    for h in range(N_ROW):
        px[h, HD:, :] = jnp.broadcast_to(dt_part[h : h + 1], (16, T)).astype(BF16)
    enter()

    odd = x % 2
    order = (2, 3 - 2 * odd, 1 + 2 * odd, 0)

    def chip(d):
        return (x + d) % N_X

    def to_sibling(part, into, ss, rs, d):
        return links.start(remote(part.at[2 * chip(d) + 1 - core], into.at[d], ss.at[d], rs.at[d], row=2 * x + 1 - core))

    def across(part, from_sibling, out, into, ss, rs, d):
        out[d] = (part[2 * chip(d) + core].astype(F32) + from_sibling[d].astype(F32)).astype(BF16)
        return links.start(remote(out.at[d], into.at[d], ss.at[d], rs.at[d], row=2 * chip(d) + core))

    def project(w, half, part):
        head = 4 * (b0 + half * (1 - 2 * b0))
        sums = dot(tok[...], w[half]).astype(BF16)
        sums = dot_t(eye[...], sums).astype(BF16)
        for h in range(4):
            part[head + h, :HD, :] = sums[h * HD : (h + 1) * HD]

    i_abc = [to_sibling(pbc, abc, abc_s, abc_r, d) for d in order]
    need(3)
    project(wx, 0, px)
    i_ax = [to_sibling(px, ax, ax_s, ax_r, d) for d in order[:2]]
    i_sbc = []
    for k, d in enumerate(order[:3]):
        links.arrive(i_abc[k])
        i_sbc.append(across(pbc, abc, sbc, rbc, sbc_s, sbc_r, d))
    need(4)
    project(wx, 1, px)
    i_ax += [to_sibling(px, ax, ax_s, ax_r, d) for d in order[2:]]
    fetch(10)
    need(5)
    project(wz, 0, pz)
    i_az = [to_sibling(pz, az, az_s, az_r, d) for d in order[:2]]
    i_sx = []
    for k, d in enumerate(order[:2]):
        links.arrive(i_ax[k])
        i_sx.append(across(px, ax, sx, rx, sx_s, sx_r, d))
    need(6)
    project(wz, 1, pz)
    i_az += [to_sibling(pz, az, az_s, az_r, d) for d in order[2:]]
    links.arrive(i_ax[2])
    i_sx.append(across(px, ax, sx, rx, sx_s, sx_r, order[2]))

    links.arrive(i_abc[3])
    bc_sum = pbc[row].astype(F32) + abc[0].astype(F32)
    for k in range(3):
        links.arrive(i_sbc[k])
    for d in range(1, N_X):
        bc_sum += rbc[d].astype(F32)
    bcraw[row] = bc_sum.astype(BF16)
    sibling = 2 * x + 1 - core

    def give(part, peer, source, ss, rs, k):
        return links.start(remote(part.at[source], part.at[source], ss.at[k], rs.at[k], row=peer))

    def gather_start(part, ss, rs):
        sent = {d: give(part, 2 * chip(d) + core, row, ss, rs, d) for d in (2, 1, 3)}
        sent[0] = give(part, sibling, row, ss, rs, 0)
        return sent

    def gather_pass_on(part, ss, rs, sent):
        for d in (1, 3, 2):
            links.arrive(sent[d])
            sent[4 + d] = give(part, sibling, 2 * chip(N_X - d) + core, ss, rs, 4 + d)

    def gather_end(sent):
        for k in (0, 5, 7, 6):
            links.arrive(sent[k])

    i_gbc = gather_start(bcraw, gbc_s, gbc_r)
    i_sz = []
    for k, d in enumerate(order[:3]):
        links.arrive(i_az[k])
        i_sz.append(across(pz, az, sz, rz, sz_s, sz_r, d))

    need(7, 8, 9)
    lanes = pl.ds(pl.multiple_of((row // 2) * 128, 128), 128)
    prm[0:4, :] = cx[:, lanes]
    prm[4:5, :] = gain[:, lanes]
    prmt[...] = prm[...].T
    col_prm = prmt[pl.ds(pl.multiple_of((row % 2) * HD, HD), HD), :]

    need(10)
    for nb_ in range(4):
        for kb in range(2):
            block = dot_t(eye[...], wout[kb * T : (kb + 1) * T, nb_ * T : (nb_ + 1) * T]).astype(BF16)
            for s in range(4):
                wt[s % 2, 2 * nb_ + s // 2, :, kb * T : (kb + 1) * T] = block[s * HD : (s + 1) * HD]

    links.arrive(i_ax[3])
    x_sum = px[row].astype(F32) + ax[0].astype(F32)
    for k in range(3):
        links.arrive(i_sx[k])
    for d in range(1, N_X):
        x_sum += rx[d].astype(F32)
    x_in = x_sum[:HD]
    xt[...] = x_in[:, 128:].astype(BF16)
    has_next, has_prior = ctx + 1 < N_CTX, ctx > 0
    present_ctx(1)
    i_xt = links.start(
        remote(xt, xt_in, tail_s.at[0], tail_r.at[0], ctx=(ctx + 1) % N_CTX), has_next, has_prior
    )

    @pl.when(ctx == 0)
    def _():
        xt_in[...] = jnp.zeros(xt_in.shape, BF16)
        bt_in[...] = jnp.zeros(bt_in.shape, BF16)

    dt_v = x_sum[HD : HD + 8] + bias_s[row]
    dt8 = jnp.maximum(dt_v, 0.0) + jnp.log1p(jnp.exp(-jnp.abs(dt_v)))
    dt_row = dt8[0:1]

    log8 = dt8 * (-decay_s[row])
    hi = log8.astype(BF16).astype(F32)
    mid = (log8 - hi).astype(BF16).astype(F32)
    low = log8 - hi - mid
    sub = iota((8, T), 0)
    three = jnp.where(sub == 0, hi, jnp.where(sub == 1, mid, jnp.where(sub == 2, low, 0.0))).astype(BF16)
    cum_row = jnp.sum(dot_t(three, tril[...]), axis=0, keepdims=True)
    cum_col = jnp.sum(dot_t(tril[...], three), axis=1, keepdims=True)
    total = cum_row[:, T - 1 :]
    tail = jnp.exp(total - cum_row)
    gap = cum_col - cum_row
    keep = iota((T, T), 0) >= iota((T, T), 1)
    weights = jnp.where(keep, jnp.exp(jnp.where(keep, gap, 0.0)), 0.0)

    gather_pass_on(bcraw, gbc_s, gbc_r, i_gbc)
    gather_end(i_gbc)
    i_bt = links.start(
        remote(bcraw.at[N_ROW - 1, pl.ds(TB - HAL, HAL)], bt_in, tail_s.at[1], tail_r.at[1], ctx=(ctx + 1) % N_CTX),
        has_next,
        has_prior,
    )

    links.arrive(i_xt)
    x_cat = jnp.concatenate([xt_in[...].astype(F32), x_in], axis=1)
    acc = col_prm[:, 3:4] * x_in
    for k in range(3):
        acc += col_prm[:, k : k + 1] * pltpu.roll(x_cat, 3 - k, 1)[:, 128:]
    x_conv = silu(acc)
    xs = x_conv * dt_row

    bcf[HAL:] = bcraw[...].reshape(T, T).astype(F32)
    links.arrive(i_bt)
    bcf[:HAL] = bt_in[...].astype(F32)
    acc = cbc[3:4, :] * bcf[HAL : HAL + T]
    for k in range(3):
        acc += cbc[k : k + 1, :] * bcf[HAL - 3 + k : HAL - 3 + k + T]
    bc_conv = silu(acc).astype(BF16)
    b_mat, c_mat = bc_conv[:, :128], bc_conv[:, 128:]

    state = dot((xs * tail).astype(BF16), b_mat)
    st[:HD] = state.astype(BF16)
    total_hi = total.astype(BF16).astype(F32)
    st[HD : HD + 8] = jnp.broadcast_to(total_hi, (8, 128)).astype(BF16)
    st[HD + 8 :] = jnp.broadcast_to(total - total_hi, (8, 128)).astype(BF16)
    i_st = {}
    for d in (2, 3, 1):
        present_ctx(d)
        copy = remote(st, sr.at[d], st_s.at[d], st_r.at[d], ctx=(ctx + d) % N_CTX)
        i_st[d] = links.start(copy, ctx + d < N_CTX, ctx >= d)

        @pl.when(ctx < d)
        def _():
            sr[d] = jnp.zeros(sr.shape[1:], BF16)

    scores = dot_t(c_mat, b_mat)
    inner = dot_t(xs.astype(BF16), (scores * weights).astype(BF16))
    partial_out = inner + skip_s[row] * x_conv
    links.arrive(i_az[3])
    z_in = pz[row].astype(F32) + az[0].astype(F32)
    for k in range(3):
        links.arrive(i_sz[k])
    for d in range(1, N_X):
        z_in += rz[d].astype(F32)
    gate = silu(z_in)
    for d in (1, 3, 2):
        links.arrive(i_st[d])

    def log_of(d):
        return (sr[d, HD : HD + 8].astype(F32) + sr[d, HD + 8 :].astype(F32))[0:1]

    enter = sr[1, :HD].astype(F32)
    enter += jnp.exp(log_of(1)) * sr[2, :HD].astype(F32)
    enter += jnp.exp(log_of(1) + log_of(2)) * sr[3, :HD].astype(F32)
    outer = dot_t(enter.astype(BF16), c_mat) * jnp.exp(cum_row)
    gated = (partial_out + outer) * gate
    inv = lax.rsqrt(jnp.sum(gated * gated, axis=0, keepdims=True) * (1.0 / HD) + 1e-05)
    nb[row] = (gated * inv * col_prm[:, 4:5]).astype(BF16)

    i_gn = gather_start(nb, gn_s, gn_r)
    gather_pass_on(nb, gn_s, gn_r, i_gn)
    gather_end(i_gn)

    heads = nb[...].reshape(N_ROW * HD, T)
    os[...] = dot(wt[1 - zl].reshape(N_Y * HD, N_ROW * HD), heads).astype(BF16).reshape(N_Y, HD, T)
    i_z, i_y = {}, {}
    for d in FAR_FIRST_Y + (0,):
        i_z[d] = links.start(remote(os.at[(y + d) % N_Y], zr.at[d], z_s.at[d], z_r.at[d], col=col + 1 - 2 * zl))
    ow[...] = dot(wt[zl].reshape(N_Y * HD, N_ROW * HD), heads).astype(BF16).reshape(N_Y, HD, T)
    present_y()
    for d in FAR_FIRST_Y:
        links.arrive(i_z[d])
        ys[d] = (ow[(y + d) % N_Y].astype(F32) + zr[d].astype(F32)).astype(BF16)
        i_y[d] = links.start(remote(ys.at[d], yr.at[d], y_s.at[d], y_r.at[d], col=((y + d) % N_Y) * 2 + zl))
    links.arrive(i_z[0])
    result = ow[y].astype(F32) + zr[0].astype(F32)
    for d in FAR_FIRST_Y:
        links.arrive(i_y[d])
        result += yr[d].astype(F32)
    out_ref[...] = result.astype(BF16)

    done()


def scratch():
    vmem = pltpu.VMEM
    dma = lambda n: pltpu.SemaphoreType.DMA((n,))
    return [
        vmem((T, KB), BF16), vmem((2, KB, T), BF16), vmem((2, KB, T), BF16),
        vmem((KB, 256), BF16), vmem((8, KB), BF16), vmem((512, KB), BF16),
        vmem((4, 512), F32), vmem((4, 256), F32), vmem((1, 512), F32),
        vmem((T, T), BF16), vmem((T, T), BF16), vmem((128, 128), F32), vmem((128, 128), F32),
        vmem((2, N_Y, HD, 512), BF16),
        *(vmem((n, rows, T), BF16) for n in (N_ROW, N_X, N_X, N_X) for rows in (TB, HD + 16, HD)),
        vmem((HD, 128), BF16), vmem((HD, 128), BF16), vmem((HAL, T), BF16),
        vmem((N_ROW, TB, T), BF16), vmem((HAL + T, T), F32),
        vmem((HD + 16, 128), BF16), vmem((N_CTX, HD + 16, 128), BF16),
        vmem((N_ROW, HD, T), BF16), vmem((N_Y, HD, T), BF16), vmem((N_Y, HD, T), BF16),
        vmem((N_Y, HD, T), BF16), vmem((N_Y, HD, T), BF16), vmem((N_Y, HD, T), BF16),
        pltpu.SemaphoreType.REGULAR, pltpu.SemaphoreType.REGULAR((N_CTX,)), dma(11), dma(2), dma(2),
        *(dma(4) for _ in range(12)),
        dma(8), dma(8), dma(4), dma(4), dma(8), dma(8), dma(8), dma(8), dma(8), dma(8),
    ]


def local(tokens, proj_x, proj_z, proj_bc, proj_dt, dt_bias, decay_rate, skip_gain, conv_x, conv_bc, norm_gain, proj_out):
    hbm = pl.BlockSpec(memory_space=pl.ANY)
    smem = pl.BlockSpec(memory_space=pltpu.SMEM)
    out = pl.pallas_call(
        kernel,
        out_shape=jax.ShapeDtypeStruct((HD, T), BF16),
        in_specs=[hbm] * 9 + [smem] * 3,
        out_specs=pl.BlockSpec(memory_space=pltpu.VMEM),
        scratch_shapes=scratch(),
        compiler_params=pltpu.CompilerParams(collective_id=0, has_side_effects=True),
    )(
        tokens, proj_x, proj_z, proj_bc, proj_dt.T, proj_out,
        conv_x.T, conv_bc.T, norm_gain.reshape(1, -1),
        dt_bias, decay_rate, skip_gain,
    )
    return out.T


def solution(mesh):
    in_specs = (
        P("ctx", "row"),
        P("row", "col"),
        P("row", "col"),
        P("row", None),
        P("row", "col"),
        P("col"),
        P("col"),
        P("col"),
        P("col", None),
        P(),
        P("col"),
        P("col", "row"),
    )
    out_specs = P("ctx", ("row", "col"))
    return jax.shard_map(local, mesh=mesh, in_specs=in_specs, out_specs=out_specs, check_vma=False)
```

```python
import functools

import jax
import jax.numpy as jnp
from jax import lax
from jax.experimental import pallas as pl
from jax.experimental.pallas import tpu as pltpu
from jax.sharding import PartitionSpec as P

MESH = pl.DeviceIdType.MESH
F32 = jnp.float32
BF16 = jnp.bfloat16

N_CTX, N_ROW, N_COL = 4, 8, 16
N_X, N_Y = 4, 8
T = 256
KB = 1024
HD = 64
TB = T // N_ROW
HAL = 16
FAR_FIRST_ROW = (4, 3, 5, 2, 6, 1, 7)
FOR_PARTNER = (4, 3, 5, 2, 6, 1, 7, 0)
FOR_OWN = (1, 7, 4, 3, 5, 2, 6, 0)


def dot(a, b):
    return jnp.dot(a, b, preferred_element_type=F32)


def dot_t(a, b):
    return lax.dot_general(a, b, (((1,), (1,)), ((), ())), preferred_element_type=F32)


def iota(shape, dim):
    return lax.broadcasted_iota(jnp.int32, shape, dim)


def rem(a, n):
    return lax.rem(a, jnp.int32(n))


def silu(v):
    return v / (1.0 + jnp.exp(-v))


class Links:
    def __init__(self):
        self.started = []

    def when(self, cond, act):
        if cond is None:
            act()
        else:
            pl.when(cond)(act)

    def start(self, copy, cond_send=None, cond_recv=None):
        self.when(cond_send, copy.start)
        self.started.append([copy, cond_send, cond_recv, True])
        return len(self.started) - 1

    def arrive(self, k):
        copy, _, cond, waiting = self.started[k]
        if waiting and cond is not False:
            self.when(cond, copy.wait_recv)
            self.started[k][3] = False

    def finish(self):
        for k, (copy, cond, _, _) in enumerate(self.started):
            self.arrive(k)
            self.when(cond, copy.wait_send)


def kernel(
    tok_h, wx_h, wz_h, wbc_h, wdt_h, wout_h, cx_h, cbc_h, gain_h,
    bias_h, decay_h, skip_h,
    out_ref,
    tok, wx, wz, wbc, wdt, wout, cx, cbc, gain,
    bias_s, decay_s, skip_s, eye, tril, prm, prmt, wt,
    pbc, px, pz, rbc, ax, az, sx, sz, rx, rz, xt, xt_in, bt_in, bcraw, bcf,
    st, sr, nb, os, ow, zr, zs, yo, yh, yv, ys, yr,
    here_y, here_ctx, sem_l, tail_s, tail_r, bt_s, bt_r,
    bc_s, bc_r, ax_s, ax_r, az_s, az_r, sx_s, sx_r, sz_s, sz_r,
    gbc_s, gbc_r, st_s, st_r, gn_s, gn_r, z_s, z_r, yo_s, yo_r, yh_s, yh_r, yv_s, yv_r, y_s, y_r,
):
    ctx = lax.axis_index("ctx")
    row = lax.axis_index("row")
    col = lax.axis_index("col")
    x, core = lax.div(row, 2), rem(row, 2)
    y, zl = lax.div(col, 2), rem(col, 2)

    def remote(src, dst, ss, rs, **peer):
        return pltpu.make_async_remote_copy(
            src_ref=src, dst_ref=dst, send_sem=ss, recv_sem=rs,
            device_id=peer, device_id_type=MESH,
        )

    barrier = pltpu.get_barrier_semaphore()

    def greet(**peer):
        pl.semaphore_signal(barrier, inc=1, device_id=peer, device_id_type=MESH)

    def rank(at):
        return jnp.minimum(at, N_Y - at) * N_Y + at

    waits = N_ROW - 1 + 1 + ctx
    for d in range(1, N_ROW):
        greet(row=rem(row + d, N_ROW))
    greet(col=col + 1 - 2 * zl)
    earlier = {}
    for d in range(1, N_Y):
        peer = rem(y + d, N_Y)
        earlier[d] = rank(peer) < rank(y)
        waits += earlier[d].astype(jnp.int32)
        pl.when(jnp.logical_not(earlier[d]))(lambda: greet(col=peer * 2 + zl))
    for d in range(1, N_CTX):
        pl.when(ctx + d < N_CTX)(lambda: greet(ctx=ctx + d))

    def enter():
        pl.semaphore_wait(barrier, waits)
        for d in range(1, N_Y):
            peer = (rem(y + d, N_Y)) * 2 + zl
            pl.when(earlier[d])(
                lambda: pl.semaphore_signal(here_y, inc=1, device_id={"col": peer}, device_id_type=MESH)
            )
        for d in range(1, N_CTX):
            pl.when(ctx >= d)(
                lambda: pl.semaphore_signal(here_ctx.at[d], inc=1, device_id={"ctx": ctx - d}, device_id_type=MESH)
            )

    def present_y():
        if not seen["y"]:
            seen["y"] = True
            later = N_Y - 1 - (waits - N_ROW - ctx)
            pl.when(later > 0)(lambda: pl.semaphore_wait(here_y, later))

    def present_ctx(d, cond):
        pl.when(cond)(lambda: pl.semaphore_wait(here_ctx.at[d], 1))

    seen = {"y": False}
    b0 = (rem(x + 2, N_X)) // 2
    cols_of = lambda b: pl.ds(pl.multiple_of(b * T, T), T)
    loads = [
        pltpu.make_async_copy(src, dst, sem_l.at[k])
        for k, (src, dst) in enumerate(
            (
                (tok_h, tok), (wbc_h, wbc), (wdt_h, wdt),
                (wx_h.at[:, cols_of(b0)], wx.at[0]), (wx_h.at[:, cols_of(1 - b0)], wx.at[1]),
                (wz_h.at[:, cols_of(b0)], wz.at[0]), (wz_h.at[:, cols_of(1 - b0)], wz.at[1]),
                (cx_h, cx), (cbc_h, cbc), (gain_h, gain), (wout_h, wout),
                (bias_h, bias_s), (decay_h, decay_s), (skip_h, skip_s),
            )
        )
    ]
    links = Links()
    pending = set()

    def fetch(*ks):
        for k in ks:
            pending.add(k)
            loads[k].start()

    fetch(0, 1, 2, 3, 4)

    def need(*ks):
        for k in ks:
            if k in pending:
                pending.remove(k)
                loads[k].wait()

    def done():
        need(*tuple(pending))
        present_y()
        links.finish()

    eye[...] = jnp.where(iota((T, T), 0) == iota((T, T), 1), 1.0, 0.0).astype(BF16)
    tril[...] = jnp.where(iota((T, T), 0) >= iota((T, T), 1), 1.0, 0.0).astype(BF16)
    prm[...] = jnp.zeros(prm.shape, F32)

    need(0, 1)
    pbc[...] = dot(tok[...], wbc[...]).astype(BF16).reshape(N_ROW, TB, T)
    fetch(5, 6, 7, 8, 9, 11, 12, 13)
    enter()
    i_bc = {}
    for d in FAR_FIRST_ROW:
        to = rem(row + d, N_ROW)
        i_bc[d] = links.start(remote(pbc.at[to], rbc.at[d], bc_s.at[d], bc_r.at[d], row=to))
    need(2)
    dt_part = dot_t(wdt[...], tok[...])
    for h in range(N_ROW):
        px[h, HD:, :] = jnp.broadcast_to(dt_part[h : h + 1], (16, T)).astype(BF16)

    odd = x % 2
    order = (2, 3 - 2 * odd, 1 + 2 * odd, 0)

    def chip(d):
        return rem(x + d, N_X)

    def to_sibling(part, into, ss, rs, d):
        return links.start(remote(part.at[2 * chip(d) + 1 - core], into.at[d], ss.at[d], rs.at[d], row=2 * x + 1 - core))

    def across(part, from_sibling, out, into, ss, rs, d):
        out[d] = (part[2 * chip(d) + core].astype(F32) + from_sibling[d].astype(F32)).astype(BF16)
        return links.start(remote(out.at[d], into.at[d], ss.at[d], rs.at[d], row=2 * chip(d) + core))

    def project(w, half, part):
        head = 4 * (b0 + half * (1 - 2 * b0))
        sums = dot(tok[...], w[half]).astype(BF16)
        sums = dot_t(eye[...], sums).astype(BF16)
        for h in range(4):
            part[head + h, :HD, :] = sums[h * HD : (h + 1) * HD]

    need(3)
    project(wx, 0, px)
    i_ax = [to_sibling(px, ax, ax_s, ax_r, d) for d in order[:2]]
    need(4)
    project(wx, 1, px)
    i_ax += [to_sibling(px, ax, ax_s, ax_r, d) for d in order[2:]]
    fetch(10)
    need(5)
    project(wz, 0, pz)
    i_az = [to_sibling(pz, az, az_s, az_r, d) for d in order[:2]]
    i_sx = []
    for k, d in enumerate(order[:2]):
        links.arrive(i_ax[k])
        i_sx.append(across(px, ax, sx, rx, sx_s, sx_r, d))
    need(6)
    project(wz, 1, pz)
    i_az += [to_sibling(pz, az, az_s, az_r, d) for d in order[2:]]
    links.arrive(i_ax[2])
    i_sx.append(across(px, ax, sx, rx, sx_s, sx_r, order[2]))

    bc_sum = pbc[row].astype(F32)
    for d in FAR_FIRST_ROW:
        links.arrive(i_bc[d])
        bc_sum += rbc[d].astype(F32)
    bcraw[row] = bc_sum.astype(BF16)
    sibling = 2 * x + 1 - core

    def give(part, peer, source, ss, rs, k):
        return links.start(remote(part.at[source], part.at[source], ss.at[k], rs.at[k], row=peer))

    def gather_start(part, ss, rs):
        sent = {d: give(part, 2 * chip(d) + core, row, ss, rs, d) for d in (2, 1, 3)}
        sent[0] = give(part, sibling, row, ss, rs, 0)
        return sent

    def gather_pass_on(part, ss, rs, sent):
        for d in (1, 3, 2):
            links.arrive(sent[d])
            sent[4 + d] = give(part, sibling, 2 * chip(N_X - d) + core, ss, rs, 4 + d)

    def gather_end(sent):
        for k in (0, 5, 7, 6):
            links.arrive(sent[k])

    i_gbc = [give(bcraw, rem(row + d, N_ROW), row, gbc_s, gbc_r, d) for d in FAR_FIRST_ROW]
    i_sz = []
    for k, d in enumerate(order[:3]):
        links.arrive(i_az[k])
        i_sz.append(across(pz, az, sz, rz, sz_s, sz_r, d))
    has_next, has_prior, last_row = ctx + 1 < N_CTX, ctx > 0, row == N_ROW - 1
    present_ctx(1, has_next & last_row)
    i_bt = []
    for to in range(N_ROW):
        copy = remote(
            bcraw.at[row, pl.ds(TB - HAL, HAL)], bt_in, bt_s.at[to], bt_r, ctx=rem(ctx + 1, N_CTX), row=to
        )
        i_bt.append(links.start(copy, has_next & last_row, has_prior if to == 0 else False))

    need(7, 8, 9, 11, 12, 13)
    lanes = pl.ds(pl.multiple_of((row // 2) * 128, 128), 128)
    prm[0:4, :] = cx[:, lanes]
    prm[4:5, :] = gain[:, lanes]
    prmt[...] = prm[...].T
    col_prm = prmt[pl.ds(pl.multiple_of((row % 2) * HD, HD), HD), :]

    need(10)
    for d in range(N_Y):
        lanes = pl.ds(pl.multiple_of((rem(y + d, N_Y)) * 128, 128), 128)
        block = dot_t(eye[:128, :128], wout[:, lanes]).astype(BF16)
        for side in range(2):
            place = jnp.where(zl == side, N_Y + FOR_OWN.index(d), FOR_PARTNER.index(d))
            wt[place] = block[side * HD : (side + 1) * HD]

    links.arrive(i_ax[3])
    x_sum = px[row].astype(F32) + ax[0].astype(F32)
    for k in range(3):
        links.arrive(i_sx[k])
    for d in range(1, N_X):
        x_sum += rx[d].astype(F32)
    x_in = x_sum[:HD]
    xt[...] = x_in[:, 128:].astype(BF16)
    present_ctx(1, has_next & jnp.logical_not(last_row))
    i_xt = links.start(
        remote(xt, xt_in, tail_s.at[0], tail_r.at[0], ctx=rem(ctx + 1, N_CTX)), has_next, has_prior
    )

    @pl.when(ctx == 0)
    def _():
        xt_in[...] = jnp.zeros(xt_in.shape, BF16)
        bt_in[...] = jnp.zeros(bt_in.shape, BF16)

    dt_v = x_sum[HD : HD + 8] + bias_s[row]
    dt8 = jnp.maximum(dt_v, 0.0) + jnp.log1p(jnp.exp(-jnp.abs(dt_v)))
    dt_row = dt8[0:1]

    log8 = dt8 * (-decay_s[row])
    hi = log8.astype(BF16).astype(F32)
    mid = (log8 - hi).astype(BF16).astype(F32)
    low = log8 - hi - mid
    sub = iota((8, T), 0)
    three = jnp.where(sub == 0, hi, jnp.where(sub == 1, mid, jnp.where(sub == 2, low, 0.0))).astype(BF16)
    cum_row = jnp.sum(dot_t(three, tril[...]), axis=0, keepdims=True)
    cum_col = jnp.sum(dot_t(tril[...], three), axis=1, keepdims=True)
    total = cum_row[:, T - 1 :]
    tail = jnp.exp(total - cum_row)
    gap = cum_col - cum_row
    keep = iota((T, T), 0) >= iota((T, T), 1)
    weights = jnp.where(keep, jnp.exp(jnp.where(keep, gap, 0.0)), 0.0)

    for k in i_gbc:
        links.arrive(k)

    links.arrive(i_xt)
    x_cat = jnp.concatenate([xt_in[...].astype(F32), x_in], axis=1)
    acc = col_prm[:, 3:4] * x_in
    for k in range(3):
        acc += col_prm[:, k : k + 1] * pltpu.roll(x_cat, 3 - k, 1)[:, 128:]
    x_conv = silu(acc)
    xs = x_conv * dt_row

    bcf[HAL:] = bcraw[...].reshape(T, T).astype(F32)
    links.arrive(i_bt[0])
    bcf[:HAL] = bt_in[...].astype(F32)
    acc = cbc[3:4, :] * bcf[HAL : HAL + T]
    for k in range(3):
        acc += cbc[k : k + 1, :] * bcf[HAL - 3 + k : HAL - 3 + k + T]
    bc_conv = silu(acc).astype(BF16)
    b_mat, c_mat = bc_conv[:, :128], bc_conv[:, 128:]

    state = dot((xs * tail).astype(BF16), b_mat)
    st[:HD] = state.astype(BF16)
    total_hi = total.astype(BF16).astype(F32)
    st[HD : HD + 8] = jnp.broadcast_to(total_hi, (8, 128)).astype(BF16)
    st[HD + 8 :] = jnp.broadcast_to(total - total_hi, (8, 128)).astype(BF16)
    i_st = {}
    for d in (2, 3, 1):
        if d > 1:
            present_ctx(d, ctx + d < N_CTX)
        copy = remote(st, sr.at[d], st_s.at[d], st_r.at[d], ctx=rem(ctx + d, N_CTX))
        i_st[d] = links.start(copy, ctx + d < N_CTX, ctx >= d)

        @pl.when(ctx < d)
        def _():
            sr[d] = jnp.zeros(sr.shape[1:], BF16)

    scores = dot_t(c_mat, b_mat)
    inner = dot_t(xs.astype(BF16), (scores * weights).astype(BF16))
    partial_out = inner + skip_s[row] * x_conv
    links.arrive(i_az[3])
    z_in = pz[row].astype(F32) + az[0].astype(F32)
    for k in range(3):
        links.arrive(i_sz[k])
    for d in range(1, N_X):
        z_in += rz[d].astype(F32)
    gate = silu(z_in)
    for d in (1, 3, 2):
        links.arrive(i_st[d])

    def log_of(d):
        return (sr[d, HD : HD + 8].astype(F32) + sr[d, HD + 8 :].astype(F32))[0:1]

    enter = sr[1, :HD].astype(F32)
    enter += jnp.exp(log_of(1)) * sr[2, :HD].astype(F32)
    enter += jnp.exp(log_of(1) + log_of(2)) * sr[3, :HD].astype(F32)
    outer = dot_t(enter.astype(BF16), c_mat) * jnp.exp(cum_row)
    gated = (partial_out + outer) * gate
    inv = lax.rsqrt(jnp.sum(gated * gated, axis=0, keepdims=True) * (1.0 / HD) + 1e-05)
    nb[row] = (gated * inv * col_prm[:, 4:5]).astype(BF16)

    i_gn = gather_start(nb, gn_s, gn_r)
    gather_pass_on(nb, gn_s, gn_r, i_gn)
    gather_end(i_gn)

    heads = nb[...].reshape(N_ROW * HD, T)

    def blocks(first, into, at):
        part = dot(wt[first : first + 4].reshape(4 * HD, N_ROW * HD), heads)
        into[at : at + 4] = part.astype(BF16).reshape(4, HD, T)

    def to_partner(src, k):
        return links.start(remote(src, zr.at[k], z_s.at[k], z_r.at[k], col=col + 1 - 2 * zl))

    def along_y_to(src, into, ss, rs, d):
        return links.start(remote(src, into, ss, rs, col=(rem(y + d, N_Y)) * 2 + zl))

    def along_y(src, into, ss, rs, d):
        return along_y_to(src, into.at[d], ss.at[d], rs.at[d], d)

    blocks(0, os, 0)
    i_z = [to_partner(os.at[k], k) for k in range(4)]
    blocks(4, os, 4)
    i_z.append(to_partner(os.at[4], 4))
    present_y()
    i_yo = [along_y(os.at[FOR_PARTNER.index(d)], yo, yo_s, yo_r, d) for d in (1, 7)]
    blocks(N_Y, ow, 0)
    i_y = [along_y(ow.at[FOR_OWN.index(d)], yr, y_s, y_r, d) for d in (1, 7)]
    blocks(N_Y + 4, ow, 4)
    i_near = {}
    for k, d in enumerate(FOR_PARTNER[:5]):
        if k == 2:
            links.arrive(i_yo[0])
            links.arrive(i_yo[1])
            zs[...] = (os[7].astype(F32) + yo[1].astype(F32) + yo[7].astype(F32)).astype(BF16)
            i_z0 = to_partner(zs, 7)
        links.arrive(i_z[k])
        own = ow[FOR_OWN.index(d)].astype(F32) + zr[k].astype(F32)
        if d not in (2, 6):
            ys[d] = own.astype(BF16)
        if d in (3, 5):
            to, on = (1, 2) if d == 3 else (7, 6)
            i_near[on] = along_y_to(ys.at[d], yv.at[on], yv_s.at[on], yv_r.at[on], to)
            continue
        if d == 4:
            i_half = {}
            for to, at in ((2, 0), (6, HD // 2)):
                rows = pl.ds(at, HD // 2)
                i_half[to] = along_y_to(ys.at[4, rows], yh.at[rows], yh_s.at[to], yh_r.at[to], to)
            continue
        if d in (2, 6):
            links.arrive(i_half[d])
            links.arrive(i_near[d])
            lo = slice(0, HD // 2), slice(HD // 2, HD)
            for side, rows in ((2, lo[0]), (6, lo[1])):
                more = own[rows] + yv[d, rows].astype(F32)
                ys[d, rows] = (more + yh[rows].astype(F32) if side == d else more).astype(BF16)
        i_y.append(along_y(ys.at[d], yr, y_s, y_r, d))
    links.arrive(i_z0)
    result = ow[7].astype(F32) + zr[7].astype(F32)
    for k in i_y:
        links.arrive(k)
    for d in (1, 2, 6, 7):
        result += yr[d].astype(F32)
    out_ref[...] = result.astype(BF16)

    done()


def scratch():
    vmem = pltpu.VMEM
    dma = lambda n: pltpu.SemaphoreType.DMA((n,))
    return [
        vmem((T, KB), BF16), vmem((2, KB, T), BF16), vmem((2, KB, T), BF16),
        vmem((KB, 256), BF16), vmem((8, KB), BF16), vmem((512, KB), BF16),
        vmem((4, 512), F32), vmem((4, 256), F32), vmem((1, 512), F32),
        pltpu.SMEM((8,), F32), pltpu.SMEM((8,), F32), pltpu.SMEM((8,), F32),
        vmem((T, T), BF16), vmem((T, T), BF16), vmem((128, 128), F32), vmem((128, 128), F32),
        vmem((2 * N_Y, HD, 512), BF16),
        vmem((N_ROW, TB, T), BF16), vmem((N_ROW, HD + 16, T), BF16), vmem((N_ROW, HD, T), BF16),
        vmem((N_ROW, TB, T), BF16),
        *(vmem((N_X, rows, T), BF16) for _ in range(3) for rows in (HD + 16, HD)),
        vmem((HD, 128), BF16), vmem((HD, 128), BF16), vmem((HAL, T), BF16),
        vmem((N_ROW, TB, T), BF16), vmem((HAL + T, T), F32),
        vmem((HD + 16, 128), BF16), vmem((N_CTX, HD + 16, 128), BF16),
        vmem((N_ROW, HD, T), BF16), vmem((N_Y, HD, T), BF16), vmem((N_Y, HD, T), BF16),
        vmem((N_Y, HD, T), BF16), vmem((HD, T), BF16), vmem((N_Y, HD, T), BF16), vmem((HD, T), BF16), vmem((N_Y, HD, T), BF16),
        vmem((N_Y, HD, T), BF16), vmem((N_Y, HD, T), BF16),
        pltpu.SemaphoreType.REGULAR, pltpu.SemaphoreType.REGULAR((N_CTX,)), dma(14), dma(1), dma(1), dma(8), pltpu.SemaphoreType.DMA,
        dma(8), dma(8), *(dma(4) for _ in range(8)),
        dma(8), dma(8), dma(4), dma(4), *(dma(8) for _ in range(12)),
    ]


def local(tokens, proj_x, proj_z, proj_bc, proj_dt, dt_bias, decay_rate, skip_gain, conv_x, conv_bc, norm_gain, proj_out):
    hbm = pl.BlockSpec(memory_space=pl.ANY)
    out = pl.pallas_call(
        kernel,
        out_shape=pltpu.VMEM((HD, T), BF16),
        in_specs=[hbm] * 12,
        scratch_shapes=scratch(),
        compiler_params=pltpu.CompilerParams(collective_id=0, has_side_effects=True),
    )(
        tokens, proj_x, proj_z, proj_bc, proj_dt.T, proj_out,
        conv_x.T, conv_bc.T, norm_gain.reshape(1, -1),
        dt_bias, decay_rate, skip_gain,
    )
    return out.T


def solution(mesh):
    in_specs = (
        P("ctx", "row"),
        P("row", "col"),
        P("row", "col"),
        P("row", None),
        P("row", "col"),
        P("col"),
        P("col"),
        P("col"),
        P("col", None),
        P(),
        P("col"),
        P("col", "row"),
    )
    out_specs = P("ctx", ("row", "col"))
    return jax.shard_map(local, mesh=mesh, in_specs=in_specs, out_specs=out_specs, check_vma=False)
```

```python
import functools

import jax
import jax.numpy as jnp
from jax import lax
from jax.experimental import pallas as pl
from jax.experimental.pallas import tpu as pltpu
from jax.sharding import PartitionSpec as P

MESH = pl.DeviceIdType.MESH
F32 = jnp.float32
BF16 = jnp.bfloat16

N_CTX, N_ROW, N_COL = 4, 8, 16
N_X, N_Y = 4, 8
T = 256
KB = 1024
HD = 64
TB = T // N_ROW
HAL = 16
FAR_FIRST_ROW = (4, 3, 5, 2, 6, 1, 7)
FOR_PARTNER = (4, 3, 5, 2, 6, 1, 7, 0)
FOR_OWN = (1, 7, 4, 3, 5, 2, 6, 0)


def dot(a, b):
    return jnp.dot(a, b, preferred_element_type=F32)


def dot_t(a, b):
    return lax.dot_general(a, b, (((1,), (1,)), ((), ())), preferred_element_type=F32)


def iota(shape, dim):
    return lax.broadcasted_iota(jnp.int32, shape, dim)


def rem(a, n):
    return lax.rem(a, jnp.int32(n))


def silu(v):
    return v / (1.0 + jnp.exp(-v))


def only_when(cond, act):
    if cond is None:
        act()
    else:
        pl.when(cond)(act)


def kernel(
    tok_h, wx_h, wz_h, wbc_h, wdt_h, wout_h, cx_h, cbc_h, gain_h,
    bias_h, decay_h, skip_h,
    out_ref,
    tok, wx, wz, wbc, wdt, wout, cx, cbc, gain,
    bias_s, decay_s, skip_s, eye, tril, prm, prmt, wt,
    pbc, px, pz, rbc, ax, az, sx, sz, rx, rz, xt, xt_in, bt_in, bcraw, bcf,
    st, sr, nb, os, ow, zr, zs, yo, yh, yv, ys, yr,
    here_y, here_ctx, sem_l,
    bc_s, ax_s, az_s, sx_s, sz_s, gbc_s, gn_s, z_s, y_s, xt_s, bt_s, st_s,
    bc_r, sx_r, sz_r, gbc_r, yo_r, y_r, xt_r, bt_r, ax_r, az_r, gn_r, z_r, yh_r, yv_r, st_r,
):
    ctx = lax.axis_index("ctx")
    row = lax.axis_index("row")
    col = lax.axis_index("col")
    x, core = lax.div(row, 2), rem(row, 2)
    y, zl = lax.div(col, 2), rem(col, 2)

    def remote(src, dst, ss, rs, **peer):
        return pltpu.make_async_remote_copy(
            src_ref=src, dst_ref=dst, send_sem=ss, recv_sem=rs,
            device_id=peer, device_id_type=MESH,
        )

    barrier = pltpu.get_barrier_semaphore()

    def greet(**peer):
        pl.semaphore_signal(barrier, inc=1, device_id=peer, device_id_type=MESH)

    def rank(at):
        return jnp.minimum(at, N_Y - at) * N_Y + at

    waits = N_ROW - 1 + 1 + ctx
    for d in range(1, N_ROW):
        greet(row=rem(row + d, N_ROW))
    greet(col=col + 1 - 2 * zl)
    earlier = {}
    for d in range(1, N_Y):
        peer = rem(y + d, N_Y)
        earlier[d] = rank(peer) < rank(y)
        waits += earlier[d].astype(jnp.int32)
        pl.when(jnp.logical_not(earlier[d]))(lambda: greet(col=peer * 2 + zl))
    for d in range(1, N_CTX):
        pl.when(ctx + d < N_CTX)(lambda: greet(ctx=ctx + d))

    def enter():
        pl.semaphore_wait(barrier, waits)
        for d in range(1, N_Y):
            peer = (rem(y + d, N_Y)) * 2 + zl
            pl.when(earlier[d])(
                lambda: pl.semaphore_signal(here_y, inc=1, device_id={"col": peer}, device_id_type=MESH)
            )
        for d in range(1, N_CTX):
            pl.when(ctx >= d)(
                lambda: pl.semaphore_signal(here_ctx.at[d], inc=1, device_id={"ctx": ctx - d}, device_id_type=MESH)
            )

    def present_y():
        if not seen["y"]:
            seen["y"] = True
            later = N_Y - 1 - (waits - N_ROW - ctx)
            pl.when(later > 0)(lambda: pl.semaphore_wait(here_y, later))

    def present_ctx(d, cond):
        pl.when(cond)(lambda: pl.semaphore_wait(here_ctx.at[d], 1))

    seen = {"y": False}
    b0 = (rem(x + 2, N_X)) // 2
    cols_of = lambda b: pl.ds(pl.multiple_of(b * T, T), T)
    loads = [
        pltpu.make_async_copy(src, dst, sem_l.at[k])
        for k, (src, dst) in enumerate(
            (
                (tok_h, tok), (wbc_h, wbc), (wdt_h, wdt),
                (wx_h.at[:, cols_of(b0)], wx.at[0]), (wx_h.at[:, cols_of(1 - b0)], wx.at[1]),
                (wz_h.at[:, cols_of(b0)], wz.at[0]), (wz_h.at[:, cols_of(1 - b0)], wz.at[1]),
                (cx_h, cx), (cbc_h, cbc), (gain_h, gain), (wout_h, wout),
                (bias_h, bias_s), (decay_h, decay_s), (skip_h, skip_s),
            )
        )
    ]
    pending = set()

    def fetch(*ks):
        for k in ks:
            pending.add(k)
            loads[k].start()

    fetch(0, 1, 2, 3, 4)

    def need(*ks):
        for k in ks:
            if k in pending:
                pending.remove(k)
                loads[k].wait()

    def begin(copy, cond_send=None, cond_recv=None):
        only_when(cond_send, copy.start)
        return copy, cond_recv

    def arrive(begun):
        copy, cond = begun
        only_when(cond, copy.wait_recv)

    def all_arrived(ref, rs):
        remote(ref, ref, rs, rs, row=sibling).wait_recv()

    def all_sent(ref, ss, cond=None):
        only_when(cond, remote(ref, ref, ss, ss, row=sibling).wait_send)

    sibling = 2 * x + 1 - core
    eye[...] = jnp.where(iota((T, T), 0) == iota((T, T), 1), 1.0, 0.0).astype(BF16)
    tril[...] = jnp.where(iota((T, T), 0) >= iota((T, T), 1), 1.0, 0.0).astype(BF16)
    prm[...] = jnp.zeros(prm.shape, F32)

    need(0, 1)
    pbc[...] = dot(tok[...], wbc[...]).astype(BF16).reshape(N_ROW, TB, T)
    fetch(5, 6, 7, 8, 9, 11, 12, 13)
    enter()
    for d in FAR_FIRST_ROW:
        to = rem(row + d, N_ROW)
        begin(remote(pbc.at[to], rbc.at[d], bc_s, bc_r, row=to))
    need(2)
    dt_part = dot_t(wdt[...], tok[...])
    for h in range(N_ROW):
        px[h, HD:, :] = jnp.broadcast_to(dt_part[h : h + 1], (16, T)).astype(BF16)

    odd = x % 2
    order = (2, 3 - 2 * odd, 1 + 2 * odd, 0)

    def chip(d):
        return rem(x + d, N_X)

    def to_sibling(part, into, ss, rs, d):
        return begin(remote(part.at[2 * chip(d) + 1 - core], into.at[d], ss, rs.at[d], row=sibling))

    def across(part, from_sibling, out, into, ss, rs, d):
        out[d] = (part[2 * chip(d) + core].astype(F32) + from_sibling[d].astype(F32)).astype(BF16)
        return begin(remote(out.at[d], into.at[d], ss, rs, row=2 * chip(d) + core))

    def project(w, half, part):
        head = 4 * (b0 + half * (1 - 2 * b0))
        sums = dot(tok[...], w[half]).astype(BF16)
        sums = dot_t(eye[...], sums).astype(BF16)
        for h in range(4):
            part[head + h, :HD] = sums[h * HD : (h + 1) * HD]

    need(3)
    project(wx, 0, px)
    i_ax = [to_sibling(px, ax, ax_s, ax_r, d) for d in order[:2]]
    need(4)
    project(wx, 1, px)
    i_ax += [to_sibling(px, ax, ax_s, ax_r, d) for d in order[2:]]
    fetch(10)
    need(5)
    project(wz, 0, pz)
    i_az = [to_sibling(pz, az, az_s, az_r, d) for d in order[:2]]
    for k, d in enumerate(order[:2]):
        arrive(i_ax[k])
        across(px, ax, sx, rx, sx_s, sx_r, d)
    need(6)
    project(wz, 1, pz)
    i_az += [to_sibling(pz, az, az_s, az_r, d) for d in order[2:]]
    arrive(i_ax[2])
    across(px, ax, sx, rx, sx_s, sx_r, order[2])

    bc_sum = pbc[row].astype(F32)
    all_arrived(rbc.at[pl.ds(1, N_ROW - 1)], bc_r)
    for d in range(1, N_ROW):
        bc_sum += rbc[d].astype(F32)
    bcraw[row] = bc_sum.astype(BF16)
    for d in FAR_FIRST_ROW:
        begin(remote(bcraw.at[row], bcraw.at[row], gbc_s, gbc_r, row=rem(row + d, N_ROW)))
    for k, d in enumerate(order[:3]):
        arrive(i_az[k])
        across(pz, az, sz, rz, sz_s, sz_r, d)
    has_next, has_prior, last_row = ctx + 1 < N_CTX, ctx > 0, row == N_ROW - 1
    present_ctx(1, has_next & last_row)
    i_bt = []
    for to in range(N_ROW):
        copy = remote(
            bcraw.at[row, pl.ds(TB - HAL, HAL)], bt_in, bt_s, bt_r, ctx=rem(ctx + 1, N_CTX), row=to
        )
        i_bt.append(begin(copy, has_next & last_row, has_prior))

    need(7, 8, 9, 11, 12, 13)
    lanes = pl.ds(pl.multiple_of((row // 2) * 128, 128), 128)
    prm[0:4, :] = cx[:, lanes]
    prm[4:5, :] = gain[:, lanes]
    prmt[...] = prm[...].T
    col_prm = prmt[pl.ds(pl.multiple_of((row % 2) * HD, HD), HD), :]

    need(10)
    for d in range(N_Y):
        lanes = pl.ds(pl.multiple_of((rem(y + d, N_Y)) * 128, 128), 128)
        block = dot_t(eye[:128, :128], wout[:, lanes]).astype(BF16)
        for side in range(2):
            place = jnp.where(zl == side, N_Y + FOR_OWN.index(d), FOR_PARTNER.index(d))
            wt[place] = block[side * HD : (side + 1) * HD]

    arrive(i_ax[3])
    x_sum = px[row].astype(F32) + ax[0].astype(F32)
    all_arrived(rx.at[pl.ds(1, N_X - 1)], sx_r)
    for d in range(1, N_X):
        x_sum += rx[d].astype(F32)
    x_in = x_sum[:HD]
    xt[...] = x_in[:, 128:].astype(BF16)
    present_ctx(1, has_next & jnp.logical_not(last_row))
    i_xt = begin(
        remote(xt, xt_in, xt_s, xt_r, ctx=rem(ctx + 1, N_CTX)), has_next, has_prior
    )

    @pl.when(ctx == 0)
    def _():
        xt_in[...] = jnp.zeros(xt_in.shape, BF16)
        bt_in[...] = jnp.zeros(bt_in.shape, BF16)

    dt_v = x_sum[HD : HD + 8] + bias_s[row]
    dt8 = jnp.maximum(dt_v, 0.0) + jnp.log1p(jnp.exp(-jnp.abs(dt_v)))
    dt_row = dt8[0:1]

    log8 = dt8 * (-decay_s[row])
    hi = log8.astype(BF16).astype(F32)
    mid = (log8 - hi).astype(BF16).astype(F32)
    low = log8 - hi - mid
    sub = iota((8, T), 0)
    three = jnp.where(sub == 0, hi, jnp.where(sub == 1, mid, jnp.where(sub == 2, low, 0.0))).astype(BF16)
    cum_row = jnp.sum(dot_t(three, tril[...]), axis=0, keepdims=True)
    cum_col = jnp.sum(dot_t(tril[...], three), axis=1, keepdims=True)
    total = cum_row[:, T - 1 :]
    tail = jnp.exp(total - cum_row)
    gap = cum_col - cum_row
    keep = iota((T, T), 0) >= iota((T, T), 1)
    weights = jnp.where(keep, jnp.exp(jnp.where(keep, gap, 0.0)), 0.0)

    all_arrived(bcraw.at[pl.ds(1, N_ROW - 1)], gbc_r)

    arrive(i_xt)
    x_cat = jnp.concatenate([xt_in[...].astype(F32), x_in], axis=1)
    acc = col_prm[:, 3:4] * x_in
    for k in range(3):
        acc += col_prm[:, k : k + 1] * pltpu.roll(x_cat, 3 - k, 1)[:, 128:]
    x_conv = silu(acc)
    xs = x_conv * dt_row

    bcf[HAL:] = bcraw[...].reshape(T, T).astype(F32)
    arrive(i_bt[0])
    bcf[:HAL] = bt_in[...].astype(F32)
    acc = cbc[3:4, :] * bcf[HAL : HAL + T]
    for k in range(3):
        acc += cbc[k : k + 1, :] * bcf[HAL - 3 + k : HAL - 3 + k + T]
    bc_conv = silu(acc).astype(BF16)
    b_mat, c_mat = bc_conv[:, :128], bc_conv[:, 128:]

    state = dot((xs * tail).astype(BF16), b_mat)
    st[:HD] = state.astype(BF16)
    total_hi = total.astype(BF16).astype(F32)
    st[HD : HD + 8] = jnp.broadcast_to(total_hi, (8, 128)).astype(BF16)
    st[HD + 8 :] = jnp.broadcast_to(total - total_hi, (8, 128)).astype(BF16)
    i_st = {}
    for d in (2, 3, 1):
        if d > 1:
            present_ctx(d, ctx + d < N_CTX)
        copy = remote(st, sr.at[d], st_s.at[d - 1], st_r.at[d - 1], ctx=rem(ctx + d, N_CTX))
        i_st[d] = begin(copy, ctx + d < N_CTX, ctx >= d)

        @pl.when(ctx < d)
        def _():
            sr[d] = jnp.zeros(sr.shape[1:], BF16)

    scores = dot_t(c_mat, b_mat)
    inner = dot_t(xs.astype(BF16), (scores * weights).astype(BF16))
    partial_out = inner + skip_s[row] * x_conv
    arrive(i_az[3])
    z_in = pz[row].astype(F32) + az[0].astype(F32)
    all_arrived(rz.at[pl.ds(1, N_X - 1)], sz_r)
    for d in range(1, N_X):
        z_in += rz[d].astype(F32)
    gate = silu(z_in)
    for d in (1, 3, 2):
        arrive(i_st[d])

    def log_of(d):
        return (sr[d, HD : HD + 8].astype(F32) + sr[d, HD + 8 :].astype(F32))[0:1]

    enter = sr[1, :HD].astype(F32)
    enter += jnp.exp(log_of(1)) * sr[2, :HD].astype(F32)
    enter += jnp.exp(log_of(1) + log_of(2)) * sr[3, :HD].astype(F32)
    outer = dot_t(enter.astype(BF16), c_mat) * jnp.exp(cum_row)
    gated = (partial_out + outer) * gate
    inv = lax.rsqrt(jnp.sum(gated * gated, axis=0, keepdims=True) * (1.0 / HD) + 1e-05)
    nb[row] = (gated * inv * col_prm[:, 4:5]).astype(BF16)

    def give(peer, source, rs):
        return begin(remote(nb.at[source], nb.at[source], gn_s, rs, row=peer))

    i_gn = {d: give(2 * chip(d) + core, row, gn_r.at[d]) for d in (2, 1, 3)}
    give(sibling, row, gn_r.at[0])
    for d in (1, 3, 2):
        arrive(i_gn[d])
        give(sibling, 2 * chip(N_X - d) + core, gn_r.at[0])
    all_arrived(nb.at[pl.ds(0, N_X)], gn_r.at[0])

    heads = nb[...].reshape(N_ROW * HD, T)

    def blocks(first, into, at):
        part = dot(wt[first : first + 4].reshape(4 * HD, N_ROW * HD), heads)
        into[at : at + 4] = part.astype(BF16).reshape(4, HD, T)

    def along_y(src, into, rs, d):
        return begin(remote(src, into, y_s, rs, col=rem(y + d, N_Y) * 2 + zl))

    halves = (slice(0, HD // 2), slice(HD // 2, HD))
    i_z = {}

    def send_z(d, side):
        k = FOR_PARTNER.index(d)
        rows = halves[side]
        i_z[d, side] = begin(
            remote(os.at[k, rows], zr.at[k, rows], z_s, z_r.at[2 * k + side], col=col + 1 - 2 * zl)
        )

    blocks(0, os, 0)
    for d, side in ((4, 0), (4, 1), (3, 0), (5, 0), (3, 1), (5, 1), (2, 0), (2, 1)):
        send_z(d, side)
    blocks(4, os, 4)
    send_z(6, 0)
    send_z(6, 1)
    present_y()
    for k, d in enumerate((1, 7)):
        along_y(os.at[FOR_PARTNER.index(d)], yo.at[k], yo_r, d)
    blocks(N_Y, ow, 0)
    for k, d in enumerate((1, 7)):
        along_y(ow.at[FOR_OWN.index(d)], yr.at[k], y_r, d)
    blocks(N_Y + 4, ow, 4)

    def pair_sum(d, side):
        arrive(i_z[d, side])
        rows = halves[side]
        return ow[FOR_OWN.index(d), rows].astype(F32) + zr[FOR_PARTNER.index(d), rows].astype(F32)

    i_half, i_near = {}, {}
    for side, to in ((0, 2), (1, 6)):
        rows = halves[side]
        ys[4, rows] = pair_sum(4, side).astype(BF16)
        i_half[to, side] = along_y(ys.at[4, rows], yh.at[rows], yh_r.at[side], to)
    for side in range(2):
        for d, to, on in ((3, 1, 2), (5, 7, 6)):
            rows, at = halves[side], (on - 2) // 4
            ys[d, rows] = pair_sum(d, side).astype(BF16)
            i_near[on, side] = along_y(ys.at[d, rows], yv.at[at, rows], yv_r.at[2 * at + side], to)
    all_arrived(yo, yo_r)
    zs[...] = (os[7].astype(F32) + yo[0].astype(F32) + yo[1].astype(F32)).astype(BF16)
    i_z0 = begin(remote(zs, zr.at[7], z_s, z_r.at[10], col=col + 1 - 2 * zl))
    for side in range(2):
        for d in (2, 6):
            rows, at = halves[side], (d - 2) // 4
            more = pair_sum(d, side)
            arrive(i_near[d, side])
            more += yv[at, rows].astype(F32)
            if (d, side) in i_half:
                arrive(i_half[d, side])
                more += yh[rows].astype(F32)
            ys[d, rows] = more.astype(BF16)
            along_y(ys.at[d, rows], yr.at[2 + at, rows], y_r, d)
    arrive(i_z0)
    result = ow[7].astype(F32) + zr[7].astype(F32)
    all_arrived(yr, y_r)
    for k in range(4):
        result += yr[k].astype(F32)
    out_ref[...] = result.astype(BF16)

    need(*tuple(pending))
    all_sent(pbc.at[pl.ds(0, 7)], bc_s)
    all_sent(px.at[pl.ds(0, 4)], ax_s)
    all_sent(pz.at[pl.ds(0, 4)], az_s)
    all_sent(sx.at[pl.ds(0, 3)], sx_s)
    all_sent(sz.at[pl.ds(0, 3)], sz_s)
    all_sent(bcraw.at[pl.ds(0, 7)], gbc_s)
    all_sent(nb.at[pl.ds(0, 7)], gn_s)
    all_sent(os.at[pl.ds(0, 6)], z_s)
    all_sent(wt.at[pl.ds(0, 9), :, pl.ds(0, T)], y_s)
    all_sent(xt, xt_s, has_next)
    all_sent(bcraw.at[pl.ds(0, 4)], bt_s, has_next & last_row)
    for d in range(1, N_CTX):
        all_sent(st, st_s.at[d - 1], ctx + d < N_CTX)


def scratch():
    vmem = pltpu.VMEM
    dma = lambda n: pltpu.SemaphoreType.DMA((n,))
    return [
        vmem((T, KB), BF16), vmem((2, KB, T), BF16), vmem((2, KB, T), BF16),
        vmem((KB, 256), BF16), vmem((8, KB), BF16), vmem((512, KB), BF16),
        vmem((4, 512), F32), vmem((4, 256), F32), vmem((1, 512), F32),
        pltpu.SMEM((8,), F32), pltpu.SMEM((8,), F32), pltpu.SMEM((8,), F32),
        vmem((T, T), BF16), vmem((T, T), BF16), vmem((128, 128), F32), vmem((128, 128), F32),
        vmem((2 * N_Y, HD, 512), BF16),
        vmem((N_ROW, TB, T), BF16), vmem((N_ROW, HD + 16, T), BF16), vmem((N_ROW, HD, T), BF16),
        vmem((N_ROW, TB, T), BF16),
        *(vmem((N_X, rows, T), BF16) for _ in range(3) for rows in (HD + 16, HD)),
        vmem((HD, 128), BF16), vmem((HD, 128), BF16), vmem((HAL, T), BF16),
        vmem((N_ROW, TB, T), BF16), vmem((HAL + T, T), F32),
        vmem((HD + 16, 128), BF16), vmem((N_CTX, HD + 16, 128), BF16),
        vmem((N_ROW, HD, T), BF16), vmem((N_Y, HD, T), BF16), vmem((N_Y, HD, T), BF16),
        vmem((N_Y, HD, T), BF16), vmem((HD, T), BF16), vmem((2, HD, T), BF16), vmem((HD, T), BF16), vmem((2, HD, T), BF16),
        vmem((N_Y, HD, T), BF16), vmem((4, HD, T), BF16),
        pltpu.SemaphoreType.REGULAR, pltpu.SemaphoreType.REGULAR((N_CTX,)), dma(14),
        *(pltpu.SemaphoreType.DMA for _ in range(11)), dma(3),
        *(pltpu.SemaphoreType.DMA for _ in range(8)), dma(4), dma(4), dma(4), dma(11), dma(2), dma(4), dma(3),
    ]


def local(tokens, proj_x, proj_z, proj_bc, proj_dt, dt_bias, decay_rate, skip_gain, conv_x, conv_bc, norm_gain, proj_out):
    hbm = pl.BlockSpec(memory_space=pl.ANY)
    out = pl.pallas_call(
        kernel,
        out_shape=pltpu.VMEM((HD, T), BF16),
        in_specs=[hbm] * 12,
        scratch_shapes=scratch(),
        compiler_params=pltpu.CompilerParams(collective_id=0, has_side_effects=True),
    )(
        tokens, proj_x, proj_z, proj_bc, proj_dt.T, proj_out,
        conv_x.T, conv_bc.T, norm_gain.reshape(1, -1),
        dt_bias, decay_rate, skip_gain,
    )
    return out.T


def solution(mesh):
    in_specs = (
        P("ctx", "row"),
        P("row", "col"),
        P("row", "col"),
        P("row", None),
        P("row", "col"),
        P("col"),
        P("col"),
        P("col"),
        P("col", None),
        P(),
        P("col"),
        P("col", "row"),
    )
    out_specs = P("ctx", ("row", "col"))
    return jax.shard_map(local, mesh=mesh, in_specs=in_specs, out_specs=out_specs, check_vma=False)
```

```python
import functools

import jax
import jax.numpy as jnp
from jax import lax
from jax.experimental import pallas as pl
from jax.experimental.pallas import tpu as pltpu
from jax.sharding import PartitionSpec as P

MESH = pl.DeviceIdType.MESH
F32 = jnp.float32
BF16 = jnp.bfloat16

N_CTX, N_ROW, N_COL = 4, 8, 16
N_X, N_Y = 4, 8
T = 256
KB = 1024
HD = 64
TB = T // N_ROW
HAL = 16
FAR_FIRST_ROW = (4, 3, 5, 2, 6, 1, 7)
FOR_PARTNER = (4, 3, 5, 2, 6, 1, 7, 0)
FOR_OWN = (1, 7, 4, 3, 5, 2, 6, 0)


def dot(a, b):
    return jnp.dot(a, b, preferred_element_type=F32)


def dot_t(a, b):
    return lax.dot_general(a, b, (((1,), (1,)), ((), ())), preferred_element_type=F32)


def iota(shape, dim):
    return lax.broadcasted_iota(jnp.int32, shape, dim)


def rem(a, n):
    return lax.rem(a, jnp.int32(n))


def silu(v):
    return v / (1.0 + jnp.exp(-v))


def only_when(cond, act):
    if cond is None:
        act()
    else:
        pl.when(cond)(act)


def kernel(
    tok_h, wx_h, wz_h, wbc_h, wdt_h, wout_h, cx_h, cbc_h, gain_h,
    bias_h, decay_h, skip_h,
    out_ref,
    tok, wx, wz, wbc, wdt, wout, cx, cbc, gain,
    bias_s, decay_s, skip_s, eye, tril, prm, prmt, wt,
    pbc, px, pz, rbc, ax, az, sx, sz, rx, rz, xt, xt_in, bt_in, bcraw, bcf,
    st, sr, nb, os, ow, zr, zs, yo, yh, yv, ys, yr,
    here_y, here_ctx, sem_l,
    bc_s, ax_s, az_s, sx_s, sz_s, gbc_s, gn_s, z_s, y_s, xt_s, bt_s, st_s,
    bc_r, sx_r, sz_r, gbc_r, yo_r, y_r, xt_r, bt_r, az_r, ax_r, gn_r, z_r, yh_r, yv_r, st_r,
):
    ctx = lax.axis_index("ctx")
    row = lax.axis_index("row")
    col = lax.axis_index("col")
    x, core = lax.div(row, 2), rem(row, 2)
    y, zl = lax.div(col, 2), rem(col, 2)

    def remote(src, dst, ss, rs, **peer):
        return pltpu.make_async_remote_copy(
            src_ref=src, dst_ref=dst, send_sem=ss, recv_sem=rs,
            device_id=peer, device_id_type=MESH,
        )

    barrier = pltpu.get_barrier_semaphore()

    def greet(**peer):
        pl.semaphore_signal(barrier, inc=1, device_id=peer, device_id_type=MESH)

    def rank(at):
        return jnp.minimum(at, N_Y - at) * N_Y + at

    waits = N_ROW - 1 + 1 + ctx
    for d in range(1, N_ROW):
        greet(row=rem(row + d, N_ROW))
    greet(col=col + 1 - 2 * zl)
    earlier = {}
    for d in range(1, N_Y):
        peer = rem(y + d, N_Y)
        earlier[d] = rank(peer) < rank(y)
        waits += earlier[d].astype(jnp.int32)
        pl.when(jnp.logical_not(earlier[d]))(lambda: greet(col=peer * 2 + zl))
    for d in range(1, N_CTX):
        pl.when(ctx + d < N_CTX)(lambda: greet(ctx=ctx + d))

    def enter():
        pl.semaphore_wait(barrier, waits)
        for d in range(1, N_Y):
            peer = (rem(y + d, N_Y)) * 2 + zl
            pl.when(earlier[d])(
                lambda: pl.semaphore_signal(here_y, inc=1, device_id={"col": peer}, device_id_type=MESH)
            )
        for d in range(1, N_CTX):
            pl.when(ctx >= d)(
                lambda: pl.semaphore_signal(here_ctx.at[d], inc=1, device_id={"ctx": ctx - d}, device_id_type=MESH)
            )

    def present_y():
        if not seen["y"]:
            seen["y"] = True
            later = N_Y - 1 - (waits - N_ROW - ctx)
            pl.when(later > 0)(lambda: pl.semaphore_wait(here_y, later))

    def present_ctx(d, cond):
        pl.when(cond)(lambda: pl.semaphore_wait(here_ctx.at[d], 1))

    seen = {"y": False}
    b0 = (rem(x + 2, N_X)) // 2
    cols_of = lambda b: pl.ds(pl.multiple_of(b * T, T), T)
    loads = [
        pltpu.make_async_copy(src, dst, sem_l.at[k])
        for k, (src, dst) in enumerate(
            (
                (tok_h, tok), (wbc_h, wbc), (wdt_h, wdt),
                (wx_h.at[:, cols_of(b0)], wx.at[0]), (wx_h.at[:, cols_of(1 - b0)], wx.at[1]),
                (wz_h.at[:, cols_of(b0)], wz.at[0]), (wz_h.at[:, cols_of(1 - b0)], wz.at[1]),
                (cx_h, cx), (cbc_h, cbc), (gain_h, gain), (wout_h, wout),
                (bias_h, bias_s), (decay_h, decay_s), (skip_h, skip_s),
            )
        )
    ]
    pending = set()

    def fetch(*ks):
        for k in ks:
            pending.add(k)
            loads[k].start()

    fetch(0, 1, 2, 3, 4)

    def need(*ks):
        for k in ks:
            if k in pending:
                pending.remove(k)
                loads[k].wait()

    def begin(copy, cond_send=None, cond_recv=None):
        only_when(cond_send, copy.start)
        return copy, cond_recv

    def arrive(begun):
        copy, cond = begun
        only_when(cond, copy.wait_recv)

    def all_arrived(ref, rs):
        remote(ref, ref, rs, rs, row=sibling).wait_recv()

    def all_sent(ref, ss, cond=None):
        only_when(cond, remote(ref, ref, ss, ss, row=sibling).wait_send)

    sibling = 2 * x + 1 - core
    eye[...] = jnp.where(iota((T, T), 0) == iota((T, T), 1), 1.0, 0.0).astype(BF16)
    tril[...] = jnp.where(iota((T, T), 0) >= iota((T, T), 1), 1.0, 0.0).astype(BF16)
    prm[...] = jnp.zeros(prm.shape, F32)

    need(0, 1)
    pbc[...] = dot(tok[...], wbc[...]).astype(BF16).reshape(N_ROW, TB, T)
    fetch(5, 6, 7, 8, 9, 11, 12, 13)
    enter()
    for d in FAR_FIRST_ROW:
        to = rem(row + d, N_ROW)
        begin(remote(pbc.at[to], rbc.at[d], bc_s, bc_r, row=to))
    need(2)
    dt_part = dot_t(wdt[...], tok[...])
    for h in range(N_ROW):
        px[h, HD:, :] = jnp.broadcast_to(dt_part[h : h + 1], (16, T)).astype(BF16)

    odd = x % 2
    order = (2, 3 - 2 * odd, 1 + 2 * odd, 0)

    def chip(d):
        return rem(x + d, N_X)

    def to_sibling(part, into, ss, rs, d):
        begin(remote(part.at[2 * chip(d) + 1 - core], into.at[d], ss, rs, row=sibling))

    def across(part, from_sibling, out, into, ss, rs, d):
        out[d] = (part[2 * chip(d) + core].astype(F32) + from_sibling[d].astype(F32)).astype(BF16)
        return begin(remote(out.at[d], into.at[d], ss, rs, row=2 * chip(d) + core))

    def project(w, half, part):
        head = 4 * (b0 + half * (1 - 2 * b0))
        sums = dot(tok[...], w[half]).astype(BF16)
        sums = dot_t(eye[...], sums).astype(BF16)
        for h in range(4):
            part[head + h, :HD] = sums[h * HD : (h + 1) * HD]

    need(3)
    project(wx, 0, px)
    for d in order[:2]:
        to_sibling(px, ax, ax_s, ax_r.at[0], d)
    need(4)
    project(wx, 1, px)
    for d in order[2:]:
        to_sibling(px, ax, ax_s, ax_r.at[1], d)
    fetch(10)
    need(5)
    project(wz, 0, pz)
    for d in order[:2]:
        to_sibling(pz, az, az_s, az_r, d)
    all_arrived(ax.at[pl.ds(0, 2)], ax_r.at[0])
    for d in order[:2]:
        across(px, ax, sx, rx, sx_s, sx_r, d)
    need(6)
    project(wz, 1, pz)
    for d in order[2:]:
        to_sibling(pz, az, az_s, az_r, d)
    all_arrived(ax.at[pl.ds(0, 2)], ax_r.at[1])
    across(px, ax, sx, rx, sx_s, sx_r, order[2])

    bc_sum = pbc[row].astype(F32)
    all_arrived(rbc.at[pl.ds(1, N_ROW - 1)], bc_r)
    for d in range(1, N_ROW):
        bc_sum += rbc[d].astype(F32)
    bcraw[row] = bc_sum.astype(BF16)
    for d in FAR_FIRST_ROW:
        begin(remote(bcraw.at[row], bcraw.at[row], gbc_s, gbc_r, row=rem(row + d, N_ROW)))
    all_arrived(az, az_r)
    for d in order[:3]:
        across(pz, az, sz, rz, sz_s, sz_r, d)
    has_next, has_prior, last_row = ctx + 1 < N_CTX, ctx > 0, row == N_ROW - 1
    present_ctx(1, has_next & last_row)
    i_bt = []
    for to in range(N_ROW):
        copy = remote(
            bcraw.at[row, pl.ds(TB - HAL, HAL)], bt_in, bt_s, bt_r, ctx=rem(ctx + 1, N_CTX), row=to
        )
        i_bt.append(begin(copy, has_next & last_row, has_prior))

    need(11, 12, 13)
    x_sum = px[row].astype(F32) + ax[0].astype(F32)
    all_arrived(rx.at[pl.ds(1, N_X - 1)], sx_r)
    for d in range(1, N_X):
        x_sum += rx[d].astype(F32)
    x_in = x_sum[:HD]
    xt[...] = x_in[:, 128:].astype(BF16)
    present_ctx(1, has_next & jnp.logical_not(last_row))
    i_xt = begin(
        remote(xt, xt_in, xt_s, xt_r, ctx=rem(ctx + 1, N_CTX)), has_next, has_prior
    )

    @pl.when(ctx == 0)
    def _():
        xt_in[...] = jnp.zeros(xt_in.shape, BF16)
        bt_in[...] = jnp.zeros(bt_in.shape, BF16)

    dt_v = x_sum[HD : HD + 8] + bias_s[row]
    dt8 = jnp.maximum(dt_v, 0.0) + jnp.log1p(jnp.exp(-jnp.abs(dt_v)))
    dt_row = dt8[0:1]

    log8 = dt8 * (-decay_s[row])
    hi = log8.astype(BF16).astype(F32)
    mid = (log8 - hi).astype(BF16).astype(F32)
    low = log8 - hi - mid
    sub = iota((8, T), 0)
    three = jnp.where(sub == 0, hi, jnp.where(sub == 1, mid, jnp.where(sub == 2, low, 0.0))).astype(BF16)
    cum_row = jnp.sum(dot_t(three, tril[...]), axis=0, keepdims=True)
    cum_col = jnp.sum(dot_t(tril[...], three), axis=1, keepdims=True)
    total = cum_row[:, T - 1 :]
    tail = jnp.exp(total - cum_row)
    gap = cum_col - cum_row
    keep = iota((T, T), 0) >= iota((T, T), 1)
    weights = jnp.where(keep, jnp.exp(jnp.where(keep, gap, 0.0)), 0.0)

    need(7, 8, 9)
    lanes = pl.ds(pl.multiple_of((row // 2) * 128, 128), 128)
    prm[0:4, :] = cx[:, lanes]
    prm[4:5, :] = gain[:, lanes]
    prmt[...] = prm[...].T
    col_prm = prmt[pl.ds(pl.multiple_of((row % 2) * HD, HD), HD), :]

    need(10)
    for d in range(N_Y):
        lanes = pl.ds(pl.multiple_of((rem(y + d, N_Y)) * 128, 128), 128)
        block = dot_t(eye[:128, :128], wout[:, lanes]).astype(BF16)
        for side in range(2):
            place = jnp.where(zl == side, N_Y + FOR_OWN.index(d), FOR_PARTNER.index(d))
            wt[place] = block[side * HD : (side + 1) * HD]

    all_arrived(bcraw.at[pl.ds(1, N_ROW - 1)], gbc_r)

    arrive(i_xt)
    x_cat = jnp.concatenate([xt_in[...].astype(F32), x_in], axis=1)
    acc = col_prm[:, 3:4] * x_in
    for k in range(3):
        acc += col_prm[:, k : k + 1] * pltpu.roll(x_cat, 3 - k, 1)[:, 128:]
    x_conv = silu(acc)
    xs = x_conv * dt_row

    bcf[HAL:] = bcraw[...].reshape(T, T).astype(F32)
    arrive(i_bt[0])
    bcf[:HAL] = bt_in[...].astype(F32)
    acc = cbc[3:4, :] * bcf[HAL : HAL + T]
    for k in range(3):
        acc += cbc[k : k + 1, :] * bcf[HAL - 3 + k : HAL - 3 + k + T]
    bc_conv = silu(acc).astype(BF16)
    b_mat, c_mat = bc_conv[:, :128], bc_conv[:, 128:]

    state = dot((xs * tail).astype(BF16), b_mat)
    st[:HD] = state.astype(BF16)
    total_hi = total.astype(BF16).astype(F32)
    st[HD : HD + 8] = jnp.broadcast_to(total_hi, (8, 128)).astype(BF16)
    st[HD + 8 :] = jnp.broadcast_to(total - total_hi, (8, 128)).astype(BF16)
    i_st = {}
    for d in (2, 3, 1):
        if d > 1:
            present_ctx(d, ctx + d < N_CTX)
        copy = remote(st, sr.at[d], st_s.at[d - 1], st_r.at[d - 1], ctx=rem(ctx + d, N_CTX))
        i_st[d] = begin(copy, ctx + d < N_CTX, ctx >= d)

        @pl.when(ctx < d)
        def _():
            sr[d] = jnp.zeros(sr.shape[1:], BF16)

    scores = dot_t(c_mat, b_mat)
    inner = dot_t(xs.astype(BF16), (scores * weights).astype(BF16))
    partial_out = inner + skip_s[row] * x_conv
    z_in = pz[row].astype(F32) + az[0].astype(F32)
    all_arrived(rz.at[pl.ds(1, N_X - 1)], sz_r)
    for d in range(1, N_X):
        z_in += rz[d].astype(F32)
    gate = silu(z_in)
    for d in (1, 3, 2):
        arrive(i_st[d])

    def log_of(d):
        return (sr[d, HD : HD + 8].astype(F32) + sr[d, HD + 8 :].astype(F32))[0:1]

    enter = sr[1, :HD].astype(F32)
    enter += jnp.exp(log_of(1)) * sr[2, :HD].astype(F32)
    enter += jnp.exp(log_of(1) + log_of(2)) * sr[3, :HD].astype(F32)
    outer = dot_t(enter.astype(BF16), c_mat) * jnp.exp(cum_row)
    gated = (partial_out + outer) * gate
    inv = lax.rsqrt(jnp.sum(gated * gated, axis=0, keepdims=True) * (1.0 / HD) + 1e-05)
    nb[row] = (gated * inv * col_prm[:, 4:5]).astype(BF16)

    def give(peer, source, rs):
        return begin(remote(nb.at[source], nb.at[source], gn_s, rs, row=peer))

    i_gn = {d: give(2 * chip(d) + core, row, gn_r.at[d]) for d in (2, 1, 3)}
    give(sibling, row, gn_r.at[0])

    all_sent(pbc.at[pl.ds(0, 7)], bc_s)
    all_sent(px.at[pl.ds(0, 4)], ax_s)
    all_sent(pz.at[pl.ds(0, 4)], az_s)
    all_sent(sx.at[pl.ds(0, 3)], sx_s)
    all_sent(sz.at[pl.ds(0, 3)], sz_s)
    all_sent(bcraw.at[pl.ds(0, 7)], gbc_s)
    all_sent(xt, xt_s, has_next)
    all_sent(bcraw.at[pl.ds(0, 4)], bt_s, has_next & last_row)
    for d in range(1, N_CTX):
        all_sent(st, st_s.at[d - 1], ctx + d < N_CTX)
    for d in (1, 3, 2):
        arrive(i_gn[d])
        give(sibling, 2 * chip(N_X - d) + core, gn_r.at[0])
    all_arrived(nb.at[pl.ds(0, N_X)], gn_r.at[0])

    heads = nb[...].reshape(N_ROW * HD, T)

    def blocks(first, into, at):
        part = dot(wt[first : first + 4].reshape(4 * HD, N_ROW * HD), heads)
        into[at : at + 4] = part.astype(BF16).reshape(4, HD, T)

    def along_y(src, into, rs, d):
        return begin(remote(src, into, y_s, rs, col=rem(y + d, N_Y) * 2 + zl))

    halves = (slice(0, HD // 2), slice(HD // 2, HD))

    def send_z(d, side):
        k, rows = FOR_PARTNER.index(d), halves[side]
        rs = z_r.at[side if d == 4 else 4 if d in (2, 6) else 2 + side]
        begin(remote(os.at[k, rows], zr.at[k, rows], z_s, rs, col=col + 1 - 2 * zl))

    blocks(0, os, 0)
    for d, side in ((4, 0), (4, 1), (3, 0), (5, 0), (3, 1), (5, 1), (2, 0), (2, 1)):
        send_z(d, side)
    blocks(4, os, 4)
    send_z(6, 0)
    send_z(6, 1)
    present_y()
    for k, d in enumerate((1, 7)):
        along_y(os.at[FOR_PARTNER.index(d)], yo.at[k], yo_r, d)
    blocks(N_Y, ow, 0)
    for k, d in enumerate((1, 7)):
        along_y(ow.at[FOR_OWN.index(d)], yr.at[k], y_r, d)
    blocks(N_Y + 4, ow, 4)
    all_sent(nb.at[pl.ds(0, 7)], gn_s)

    def pair_sum(d, side):
        rows = halves[side]
        return ow[FOR_OWN.index(d), rows].astype(F32) + zr[FOR_PARTNER.index(d), rows].astype(F32)

    i_half, i_near = {}, {}
    for side, to in ((0, 2), (1, 6)):
        rows = halves[side]
        all_arrived(zr.at[0, rows], z_r.at[side])
        ys[4, rows] = pair_sum(4, side).astype(BF16)
        i_half[to, side] = along_y(ys.at[4, rows], yh.at[rows], yh_r.at[side], to)
    for side in range(2):
        all_arrived(zr.at[0], z_r.at[2 + side])
        for d, to, on in ((3, 1, 2), (5, 7, 6)):
            rows, at = halves[side], (on - 2) // 4
            ys[d, rows] = pair_sum(d, side).astype(BF16)
            i_near[on, side] = along_y(ys.at[d, rows], yv.at[at, rows], yv_r.at[2 * at + side], to)
    all_arrived(yo, yo_r)
    zs[...] = (os[7].astype(F32) + yo[0].astype(F32) + yo[1].astype(F32)).astype(BF16)
    i_z0 = begin(remote(zs, zr.at[7], z_s, z_r.at[5], col=col + 1 - 2 * zl))
    all_arrived(zr.at[pl.ds(0, 2)], z_r.at[4])
    for side in range(2):
        for d in (2, 6):
            rows, at = halves[side], (d - 2) // 4
            more = pair_sum(d, side)
            arrive(i_near[d, side])
            more += yv[at, rows].astype(F32)
            if (d, side) in i_half:
                arrive(i_half[d, side])
                more += yh[rows].astype(F32)
            ys[d, rows] = more.astype(BF16)
            along_y(ys.at[d, rows], yr.at[2 + at, rows], y_r, d)
    arrive(i_z0)
    result = ow[7].astype(F32) + zr[7].astype(F32)
    all_arrived(yr, y_r)
    for k in range(4):
        result += yr[k].astype(F32)
    out_ref[...] = result.astype(BF16)

    need(*tuple(pending))
    all_sent(os.at[pl.ds(0, 6)], z_s)
    all_sent(wt.at[pl.ds(0, 9), :, pl.ds(0, T)], y_s)


def scratch():
    vmem = pltpu.VMEM
    dma = lambda n: pltpu.SemaphoreType.DMA((n,))
    return [
        vmem((T, KB), BF16), vmem((2, KB, T), BF16), vmem((2, KB, T), BF16),
        vmem((KB, 256), BF16), vmem((8, KB), BF16), vmem((512, KB), BF16),
        vmem((4, 512), F32), vmem((4, 256), F32), vmem((1, 512), F32),
        pltpu.SMEM((8,), F32), pltpu.SMEM((8,), F32), pltpu.SMEM((8,), F32),
        vmem((T, T), BF16), vmem((T, T), BF16), vmem((128, 128), F32), vmem((128, 128), F32),
        vmem((2 * N_Y, HD, 512), BF16),
        vmem((N_ROW, TB, T), BF16), vmem((N_ROW, HD + 16, T), BF16), vmem((N_ROW, HD, T), BF16),
        vmem((N_ROW, TB, T), BF16),
        *(vmem((N_X, rows, T), BF16) for _ in range(3) for rows in (HD + 16, HD)),
        vmem((HD, 128), BF16), vmem((HD, 128), BF16), vmem((HAL, T), BF16),
        vmem((N_ROW, TB, T), BF16), vmem((HAL + T, T), F32),
        vmem((HD + 16, 128), BF16), vmem((N_CTX, HD + 16, 128), BF16),
        vmem((N_ROW, HD, T), BF16), vmem((N_Y, HD, T), BF16), vmem((N_Y, HD, T), BF16),
        vmem((N_Y, HD, T), BF16), vmem((HD, T), BF16), vmem((2, HD, T), BF16), vmem((HD, T), BF16), vmem((2, HD, T), BF16),
        vmem((N_Y, HD, T), BF16), vmem((4, HD, T), BF16),
        pltpu.SemaphoreType.REGULAR, pltpu.SemaphoreType.REGULAR((N_CTX,)), dma(14),
        *(pltpu.SemaphoreType.DMA for _ in range(11)), dma(3),
        *(pltpu.SemaphoreType.DMA for _ in range(9)), dma(2), dma(4), dma(6), dma(2), dma(4), dma(3),
    ]


def local(tokens, proj_x, proj_z, proj_bc, proj_dt, dt_bias, decay_rate, skip_gain, conv_x, conv_bc, norm_gain, proj_out):
    hbm = pl.BlockSpec(memory_space=pl.ANY)
    out = pl.pallas_call(
        kernel,
        out_shape=pltpu.VMEM((HD, T), BF16),
        in_specs=[hbm] * 12,
        scratch_shapes=scratch(),
        compiler_params=pltpu.CompilerParams(collective_id=0, has_side_effects=True),
    )(
        tokens, proj_x, proj_z, proj_bc, proj_dt.T, proj_out,
        conv_x.T, conv_bc.T, norm_gain.reshape(1, -1),
        dt_bias, decay_rate, skip_gain,
    )
    return out.T


def solution(mesh):
    in_specs = (
        P("ctx", "row"),
        P("row", "col"),
        P("row", "col"),
        P("row", None),
        P("row", "col"),
        P("col"),
        P("col"),
        P("col"),
        P("col", None),
        P(),
        P("col"),
        P("col", "row"),
    )
    out_specs = P("ctx", ("row", "col"))
    return jax.shard_map(local, mesh=mesh, in_specs=in_specs, out_specs=out_specs, check_vma=False)
```

```python
import functools

import jax
import jax.numpy as jnp
from jax import lax
from jax.experimental import pallas as pl
from jax.experimental.pallas import tpu as pltpu
from jax.sharding import PartitionSpec as P

MESH = pl.DeviceIdType.MESH
F32 = jnp.float32
BF16 = jnp.bfloat16

N_CTX, N_ROW, N_COL = 4, 8, 16
N_X, N_Y = 4, 8
T = 256
KB = 1024
HD = 64
TB = T // N_ROW
HAL = 16
FAR_FIRST_ROW = (4, 3, 5, 2, 6, 1, 7)
FOR_PARTNER = (4, 3, 5, 2, 6, 1, 7, 0)
FOR_OWN = (1, 7, 4, 3, 5, 2, 6, 0)


def dot(a, b):
    return jnp.dot(a, b, preferred_element_type=F32)


def dot_t(a, b):
    return lax.dot_general(a, b, (((1,), (1,)), ((), ())), preferred_element_type=F32)


def iota(shape, dim):
    return lax.broadcasted_iota(jnp.int32, shape, dim)


def rem(a, n):
    return lax.rem(a, jnp.int32(n))


def silu(v):
    return v / (1.0 + jnp.exp(-v))


def only_when(cond, act):
    if cond is None:
        act()
    else:
        pl.when(cond)(act)


def kernel(
    tok_h, wx_h, wz_h, wbc_h, wdt_h, wout_h, cx_h, cbc_h, gain_h,
    bias_h, decay_h, skip_h,
    out_ref,
    tok, wx, wz, wbc, wdt, wout, cx, cbc, gain,
    bias_s, decay_s, skip_s, eye, tril, prm, prmt, wt,
    pbc, px, pz, rbc, ax, az, sx, sz, rx, rz, xt, xt_in, bt_in, bcraw, bcf,
    st, sr, nb, os, ow, zr, zs, yo, yh, yv, ys, yr,
    here_y, here_ctx, sem_l,
    bc_s, ax_s, az_s, sx_s, sz_s, gbc_s, gn_s, z_s, y_s, xt_s, bt_s, st_s,
    bc_r, sx_r, sz_r, gbc_r, yo_r, y_r, xt_r, bt_r, az_r, ax_r, gn_r, z_r, yh_r, yv_r, st_r,
):
    ctx = lax.axis_index("ctx")
    row = lax.axis_index("row")
    col = lax.axis_index("col")
    x, core = lax.div(row, 2), rem(row, 2)
    y, zl = lax.div(col, 2), rem(col, 2)

    def remote(src, dst, ss, rs, **peer):
        return pltpu.make_async_remote_copy(
            src_ref=src, dst_ref=dst, send_sem=ss, recv_sem=rs,
            device_id=peer, device_id_type=MESH,
        )

    barrier = pltpu.get_barrier_semaphore()

    def greet(**peer):
        pl.semaphore_signal(barrier, inc=1, device_id=peer, device_id_type=MESH)

    def rank(at):
        return jnp.minimum(at, N_Y - at) * N_Y + at

    waits = N_ROW - 1 + 1 + ctx
    for d in range(1, N_ROW):
        greet(row=rem(row + d, N_ROW))
    greet(col=col + 1 - 2 * zl)
    earlier = {}
    for d in range(1, N_Y):
        peer = rem(y + d, N_Y)
        earlier[d] = rank(peer) < rank(y)
        waits += earlier[d].astype(jnp.int32)
        pl.when(jnp.logical_not(earlier[d]))(lambda: greet(col=peer * 2 + zl))
    for d in range(1, N_CTX):
        pl.when(ctx + d < N_CTX)(lambda: greet(ctx=ctx + d))

    def enter():
        pl.semaphore_wait(barrier, waits)
        for d in range(1, N_Y):
            peer = (rem(y + d, N_Y)) * 2 + zl
            pl.when(earlier[d])(
                lambda: pl.semaphore_signal(here_y, inc=1, device_id={"col": peer}, device_id_type=MESH)
            )
        for d in range(1, N_CTX):
            pl.when(ctx >= d)(
                lambda: pl.semaphore_signal(here_ctx.at[d], inc=1, device_id={"ctx": ctx - d}, device_id_type=MESH)
            )

    def present_y():
        if not seen["y"]:
            seen["y"] = True
            later = N_Y - 1 - (waits - N_ROW - ctx)
            pl.when(later > 0)(lambda: pl.semaphore_wait(here_y, later))

    def present_ctx(d, cond):
        pl.when(cond)(lambda: pl.semaphore_wait(here_ctx.at[d], 1))

    seen = {"y": False}
    b0 = (rem(x + 2, N_X)) // 2
    cols_of = lambda b: pl.ds(pl.multiple_of(b * T, T), T)
    loads = [
        pltpu.make_async_copy(src, dst, sem_l.at[k])
        for k, (src, dst) in enumerate(
            (
                (tok_h, tok), (wbc_h, wbc), (wdt_h, wdt),
                (wx_h.at[:, cols_of(b0)], wx.at[0]), (wx_h.at[:, cols_of(1 - b0)], wx.at[1]),
                (wz_h.at[:, cols_of(b0)], wz.at[0]), (wz_h.at[:, cols_of(1 - b0)], wz.at[1]),
                (cx_h, cx), (cbc_h, cbc), (gain_h, gain), (wout_h, wout),
                (bias_h, bias_s), (decay_h, decay_s), (skip_h, skip_s),
            )
        )
    ]
    pending = set()

    def fetch(*ks):
        for k in ks:
            pending.add(k)
            loads[k].start()

    fetch(0, 1, 2, 3, 4)

    def need(*ks):
        for k in ks:
            if k in pending:
                pending.remove(k)
                loads[k].wait()

    def begin(copy, cond_send=None, cond_recv=None):
        only_when(cond_send, copy.start)
        return copy, cond_recv

    def arrive(begun):
        copy, cond = begun
        only_when(cond, copy.wait_recv)

    def all_arrived(ref, rs):
        remote(ref, ref, rs, rs, row=sibling).wait_recv()

    def all_sent(ref, ss, cond=None):
        only_when(cond, remote(ref, ref, ss, ss, row=sibling).wait_send)

    sibling = 2 * x + 1 - core
    eye[...] = jnp.where(iota((T, T), 0) == iota((T, T), 1), 1.0, 0.0).astype(BF16)
    tril[...] = jnp.where(iota((T, T), 0) >= iota((T, T), 1), 1.0, 0.0).astype(BF16)
    prm[...] = jnp.zeros(prm.shape, F32)

    need(0, 1)
    pbc[...] = dot(tok[...], wbc[...]).astype(BF16).reshape(N_ROW, TB, T)
    fetch(5, 6, 7, 8, 9, 11, 12, 13)
    enter()
    for d in FAR_FIRST_ROW:
        to = rem(row + d, N_ROW)
        begin(remote(pbc.at[to], rbc.at[d], bc_s, bc_r, row=to))
    need(2)
    dt_part = dot_t(wdt[...], tok[...])
    for h in range(N_ROW):
        px[h, HD:, :] = jnp.broadcast_to(dt_part[h : h + 1], (16, T)).astype(BF16)

    odd = x % 2
    order = (2, 3 - 2 * odd, 1 + 2 * odd, 0)

    def chip(d):
        return rem(x + d, N_X)

    def to_sibling(part, into, ss, rs, d):
        begin(remote(part.at[2 * chip(d) + 1 - core], into.at[d], ss, rs, row=sibling))

    def across(part, from_sibling, out, into, ss, rs, d):
        out[d] = (part[2 * chip(d) + core].astype(F32) + from_sibling[d].astype(F32)).astype(BF16)
        return begin(remote(out.at[d], into.at[d], ss, rs, row=2 * chip(d) + core))

    def project(w, half, part):
        head = 4 * (b0 + half * (1 - 2 * b0))
        sums = dot(tok[...], w[half]).astype(BF16)
        sums = dot_t(eye[...], sums).astype(BF16)
        for h in range(4):
            part[head + h, :HD] = sums[h * HD : (h + 1) * HD]

    need(3)
    project(wx, 0, px)
    for d in order[:2]:
        to_sibling(px, ax, ax_s, ax_r.at[0], d)
    need(4)
    project(wx, 1, px)
    for d in order[2:]:
        to_sibling(px, ax, ax_s, ax_r.at[1], d)
    fetch(10)
    need(5)
    project(wz, 0, pz)
    for d in order[:2]:
        to_sibling(pz, az, az_s, az_r, d)
    all_arrived(ax.at[pl.ds(0, 2)], ax_r.at[0])
    for d in order[:2]:
        across(px, ax, sx, rx, sx_s, sx_r, d)
    need(6)
    project(wz, 1, pz)
    for d in order[2:]:
        to_sibling(pz, az, az_s, az_r, d)
    all_arrived(ax.at[pl.ds(0, 2)], ax_r.at[1])
    across(px, ax, sx, rx, sx_s, sx_r, order[2])

    bc_sum = pbc[row].astype(F32)
    all_arrived(rbc.at[pl.ds(1, N_ROW - 1)], bc_r)
    for d in range(1, N_ROW):
        bc_sum += rbc[d].astype(F32)
    bcraw[row] = bc_sum.astype(BF16)
    for d in FAR_FIRST_ROW:
        begin(remote(bcraw.at[row], bcraw.at[row], gbc_s, gbc_r, row=rem(row + d, N_ROW)))
    all_arrived(az, az_r)
    for d in order[:3]:
        across(pz, az, sz, rz, sz_s, sz_r, d)
    has_next, has_prior, last_row = ctx + 1 < N_CTX, ctx > 0, row == N_ROW - 1
    present_ctx(1, has_next & last_row)
    i_bt = []
    for to in range(N_ROW):
        copy = remote(
            bcraw.at[row, pl.ds(TB - HAL, HAL)], bt_in, bt_s, bt_r, ctx=rem(ctx + 1, N_CTX), row=to
        )
        i_bt.append(begin(copy, has_next & last_row, has_prior))

    need(11, 12, 13)
    x_sum = px[row].astype(F32) + ax[0].astype(F32)
    all_arrived(rx.at[pl.ds(1, N_X - 1)], sx_r)
    for d in range(1, N_X):
        x_sum += rx[d].astype(F32)
    x_in = x_sum[:HD]
    xt[...] = x_in[:, 128:].astype(BF16)
    present_ctx(1, has_next & jnp.logical_not(last_row))
    i_xt = begin(
        remote(xt, xt_in, xt_s, xt_r, ctx=rem(ctx + 1, N_CTX)), has_next, has_prior
    )

    @pl.when(ctx == 0)
    def _():
        xt_in[...] = jnp.zeros(xt_in.shape, BF16)
        bt_in[...] = jnp.zeros(bt_in.shape, BF16)

    dt_v = x_sum[HD : HD + 8] + bias_s[row]
    dt8 = jnp.maximum(dt_v, 0.0) + jnp.log1p(jnp.exp(-jnp.abs(dt_v)))
    dt_row = dt8[0:1]

    log8 = dt8 * (-decay_s[row])
    hi = log8.astype(BF16).astype(F32)
    mid = (log8 - hi).astype(BF16).astype(F32)
    low = log8 - hi - mid
    sub = iota((8, T), 0)
    three = jnp.where(sub == 0, hi, jnp.where(sub == 1, mid, jnp.where(sub == 2, low, 0.0))).astype(BF16)
    cum_row = jnp.sum(dot_t(three, tril[...]), axis=0, keepdims=True)
    cum_col = jnp.sum(dot_t(tril[...], three), axis=1, keepdims=True)
    total = cum_row[:, T - 1 :]
    tail = jnp.exp(total - cum_row)
    gap = cum_col - cum_row
    keep = iota((T, T), 0) >= iota((T, T), 1)
    weights = jnp.where(keep, jnp.exp(jnp.where(keep, gap, 0.0)), 0.0)

    need(7, 8, 9)
    lanes = pl.ds(pl.multiple_of((row // 2) * 128, 128), 128)
    prm[0:4, :] = cx[:, lanes]
    prm[4:5, :] = gain[:, lanes]
    prmt[...] = prm[...].T
    col_prm = prmt[pl.ds(pl.multiple_of((row % 2) * HD, HD), HD), :]

    need(10)
    for d in range(N_Y):
        lanes = pl.ds(pl.multiple_of((rem(y + d, N_Y)) * 128, 128), 128)
        block = dot_t(eye[:128, :128], wout[:, lanes]).astype(BF16)
        for side in range(2):
            place = jnp.where(zl == side, N_Y + FOR_OWN.index(d), FOR_PARTNER.index(d))
            wt[place] = block[side * HD : (side + 1) * HD]

    all_arrived(bcraw.at[pl.ds(1, N_ROW - 1)], gbc_r)

    arrive(i_xt)
    x_cat = jnp.concatenate([xt_in[...].astype(F32), x_in], axis=1)
    acc = col_prm[:, 3:4] * x_in
    for k in range(3):
        acc += col_prm[:, k : k + 1] * pltpu.roll(x_cat, 3 - k, 1)[:, 128:]
    x_conv = silu(acc)
    xs = x_conv * dt_row

    bcf[HAL:] = bcraw[...].reshape(T, T).astype(F32)
    arrive(i_bt[0])
    bcf[:HAL] = bt_in[...].astype(F32)
    acc = cbc[3:4, :] * bcf[HAL : HAL + T]
    for k in range(3):
        acc += cbc[k : k + 1, :] * bcf[HAL - 3 + k : HAL - 3 + k + T]
    bc_conv = silu(acc).astype(BF16)
    b_mat, c_mat = bc_conv[:, :128], bc_conv[:, 128:]

    state = dot((xs * tail).astype(BF16), b_mat)
    st[:HD] = state.astype(BF16)
    total_hi = total.astype(BF16).astype(F32)
    st[HD : HD + 8] = jnp.broadcast_to(total_hi, (8, 128)).astype(BF16)
    st[HD + 8 :] = jnp.broadcast_to(total - total_hi, (8, 128)).astype(BF16)
    i_st = {}
    for d in (2, 3, 1):
        if d > 1:
            present_ctx(d, ctx + d < N_CTX)
        copy = remote(st, sr.at[d], st_s.at[d - 1], st_r.at[d - 1], ctx=rem(ctx + d, N_CTX))
        i_st[d] = begin(copy, ctx + d < N_CTX, ctx >= d)

        @pl.when(ctx < d)
        def _():
            sr[d] = jnp.zeros(sr.shape[1:], BF16)

    scores = dot_t(c_mat, b_mat)
    inner = dot_t(xs.astype(BF16), (scores * weights).astype(BF16))
    partial_out = inner + skip_s[row] * x_conv
    z_in = pz[row].astype(F32) + az[0].astype(F32)
    all_arrived(rz.at[pl.ds(1, N_X - 1)], sz_r)
    for d in range(1, N_X):
        z_in += rz[d].astype(F32)
    gate = silu(z_in)
    for d in (1, 3, 2):
        arrive(i_st[d])

    def log_of(d):
        return (sr[d, HD : HD + 8].astype(F32) + sr[d, HD + 8 :].astype(F32))[0:1]

    enter = sr[1, :HD].astype(F32)
    enter += jnp.exp(log_of(1)) * sr[2, :HD].astype(F32)
    enter += jnp.exp(log_of(1) + log_of(2)) * sr[3, :HD].astype(F32)
    outer = dot_t(enter.astype(BF16), c_mat) * jnp.exp(cum_row)
    gated = (partial_out + outer) * gate
    inv = lax.rsqrt(jnp.sum(gated * gated, axis=0, keepdims=True) * (1.0 / HD) + 1e-05)
    nb[row] = (gated * inv * col_prm[:, 4:5]).astype(BF16)

    def give(peer, source, rs):
        return begin(remote(nb.at[source], nb.at[source], gn_s, rs, row=peer))

    i_gn = {d: give(2 * chip(d) + core, row, gn_r.at[d]) for d in (2, 1, 3)}
    give(sibling, row, gn_r.at[0])

    all_sent(pbc.at[pl.ds(0, 7)], bc_s)
    all_sent(px.at[pl.ds(0, 4)], ax_s)
    all_sent(pz.at[pl.ds(0, 4)], az_s)
    all_sent(sx.at[pl.ds(0, 3)], sx_s)
    all_sent(sz.at[pl.ds(0, 3)], sz_s)
    all_sent(bcraw.at[pl.ds(0, 7)], gbc_s)
    all_sent(xt, xt_s, has_next)
    all_sent(bcraw.at[pl.ds(0, 4)], bt_s, has_next & last_row)
    for d in range(1, N_CTX):
        all_sent(st, st_s.at[d - 1], ctx + d < N_CTX)
    for d in (1, 3, 2):
        arrive(i_gn[d])
        give(sibling, 2 * chip(N_X - d) + core, gn_r.at[0])
    all_arrived(nb.at[pl.ds(0, N_X)], gn_r.at[0])

    heads = nb[...].reshape(N_ROW * HD, T)

    def blocks(first, into, at):
        part = dot(wt[first : first + 4].reshape(4 * HD, N_ROW * HD), heads)
        into[at : at + 4] = part.astype(BF16).reshape(4, HD, T)

    def along_y(src, into, rs, d):
        return begin(remote(src, into, y_s, rs, col=rem(y + d, N_Y) * 2 + zl))

    halves = (slice(0, HD // 2), slice(HD // 2, HD))

    def send_z(d, side):
        k, rows = FOR_PARTNER.index(d), slice(0, HD) if d in (2, 6) else halves[side]
        rs = z_r.at[side if d == 4 else 4 if d in (2, 6) else 2 + side]
        begin(remote(os.at[k, rows], zr.at[k, rows], z_s, rs, col=col + 1 - 2 * zl))

    blocks(0, os, 0)
    for d, side in ((4, 0), (4, 1), (3, 0), (5, 0), (3, 1), (5, 1), (2, 0)):
        send_z(d, side)
    blocks(4, os, 4)
    send_z(6, 0)
    present_y()
    for k, d in enumerate((1, 7)):
        along_y(os.at[FOR_PARTNER.index(d)], yo.at[k], yo_r, d)
    blocks(N_Y, ow, 0)
    for k, d in enumerate((1, 7)):
        along_y(ow.at[FOR_OWN.index(d)], yr.at[k], y_r, d)
    blocks(N_Y + 4, ow, 4)
    all_sent(nb.at[pl.ds(0, 7)], gn_s)

    def pair_sum(d, side):
        rows = halves[side]
        return ow[FOR_OWN.index(d), rows].astype(F32) + zr[FOR_PARTNER.index(d), rows].astype(F32)

    i_half, i_near = {}, {}
    for side, to in ((0, 2), (1, 6)):
        rows = halves[side]
        all_arrived(zr.at[0, rows], z_r.at[side])
        ys[4, rows] = pair_sum(4, side).astype(BF16)
        i_half[to, side] = along_y(ys.at[4, rows], yh.at[rows], yh_r.at[side], to)
    for side in range(2):
        all_arrived(zr.at[0], z_r.at[2 + side])
        for d, to, on in ((3, 1, 2), (5, 7, 6)):
            rows, at = halves[side], (on - 2) // 4
            ys[d, rows] = pair_sum(d, side).astype(BF16)
            i_near[on, side] = along_y(ys.at[d, rows], yv.at[at, rows], yv_r.at[2 * at + side], to)
    all_arrived(yo, yo_r)
    zs[...] = (os[7].astype(F32) + yo[0].astype(F32) + yo[1].astype(F32)).astype(BF16)
    i_z0 = begin(remote(zs, zr.at[7], z_s, z_r.at[5], col=col + 1 - 2 * zl))
    all_arrived(zr.at[pl.ds(0, 2)], z_r.at[4])
    for side in range(2):
        for d in (2, 6):
            rows, at = halves[side], (d - 2) // 4
            more = pair_sum(d, side)
            arrive(i_near[d, side])
            more += yv[at, rows].astype(F32)
            if (d, side) in i_half:
                arrive(i_half[d, side])
                more += yh[rows].astype(F32)
            ys[d, rows] = more.astype(BF16)
            along_y(ys.at[d, rows], yr.at[2 + at, rows], y_r, d)
    arrive(i_z0)
    result = ow[7].astype(F32) + zr[7].astype(F32)
    all_arrived(yr, y_r)
    for k in range(4):
        result += yr[k].astype(F32)
    out_ref[...] = result.astype(BF16)

    need(*tuple(pending))
    all_sent(os.at[pl.ds(0, 6)], z_s)
    all_sent(wt.at[pl.ds(0, 9), :, pl.ds(0, T)], y_s)


def scratch():
    vmem = pltpu.VMEM
    dma = lambda n: pltpu.SemaphoreType.DMA((n,))
    return [
        vmem((T, KB), BF16), vmem((2, KB, T), BF16), vmem((2, KB, T), BF16),
        vmem((KB, 256), BF16), vmem((8, KB), BF16), vmem((512, KB), BF16),
        vmem((4, 512), F32), vmem((4, 256), F32), vmem((1, 512), F32),
        pltpu.SMEM((8,), F32), pltpu.SMEM((8,), F32), pltpu.SMEM((8,), F32),
        vmem((T, T), BF16), vmem((T, T), BF16), vmem((128, 128), F32), vmem((128, 128), F32),
        vmem((2 * N_Y, HD, 512), BF16),
        vmem((N_ROW, TB, T), BF16), vmem((N_ROW, HD + 16, T), BF16), vmem((N_ROW, HD, T), BF16),
        vmem((N_ROW, TB, T), BF16),
        *(vmem((N_X, rows, T), BF16) for _ in range(3) for rows in (HD + 16, HD)),
        vmem((HD, 128), BF16), vmem((HD, 128), BF16), vmem((HAL, T), BF16),
        vmem((N_ROW, TB, T), BF16), vmem((HAL + T, T), F32),
        vmem((HD + 16, 128), BF16), vmem((N_CTX, HD + 16, 128), BF16),
        vmem((N_ROW, HD, T), BF16), vmem((N_Y, HD, T), BF16), vmem((N_Y, HD, T), BF16),
        vmem((N_Y, HD, T), BF16), vmem((HD, T), BF16), vmem((2, HD, T), BF16), vmem((HD, T), BF16), vmem((2, HD, T), BF16),
        vmem((N_Y, HD, T), BF16), vmem((4, HD, T), BF16),
        pltpu.SemaphoreType.REGULAR, pltpu.SemaphoreType.REGULAR((N_CTX,)), dma(14),
        *(pltpu.SemaphoreType.DMA for _ in range(11)), dma(3),
        *(pltpu.SemaphoreType.DMA for _ in range(9)), dma(2), dma(4), dma(6), dma(2), dma(4), dma(3),
    ]


def local(tokens, proj_x, proj_z, proj_bc, proj_dt, dt_bias, decay_rate, skip_gain, conv_x, conv_bc, norm_gain, proj_out):
    hbm = pl.BlockSpec(memory_space=pl.ANY)
    out = pl.pallas_call(
        kernel,
        out_shape=pltpu.VMEM((HD, T), BF16),
        in_specs=[hbm] * 12,
        scratch_shapes=scratch(),
        compiler_params=pltpu.CompilerParams(collective_id=0, has_side_effects=True),
    )(
        tokens, proj_x, proj_z, proj_bc, proj_dt.T, proj_out,
        conv_x.T, conv_bc.T, norm_gain.reshape(1, -1),
        dt_bias, decay_rate, skip_gain,
    )
    return out.T


def solution(mesh):
    in_specs = (
        P("ctx", "row"),
        P("row", "col"),
        P("row", "col"),
        P("row", None),
        P("row", "col"),
        P("col"),
        P("col"),
        P("col"),
        P("col", None),
        P(),
        P("col"),
        P("col", "row"),
    )
    out_specs = P("ctx", ("row", "col"))
    return jax.shard_map(local, mesh=mesh, in_specs=in_specs, out_specs=out_specs, check_vma=False)
```
